32 devices in a mesh: tiles: 1, rows: 32 (over z, y, x, core).
Axes of the slice: x: 2, y: 2, z: 4, core: 2. Of those that a mesh axis runs over, the one named last changes fastest.
Arguments:
- features: bfloat16 [512, 512, 256], P(('tiles', 'rows')), may hold values from -6 to 6
- corners: int32 [256, 2], P(('tiles', 'rows')), may hold values from 0 to 511, as said below
- offsets: int32 [256, 1], P(('tiles', 'rows')), may hold values from 0 to 3; in each aligned block of 8 rows (0 to 7, 8 to 15, ...) at most 2 rows name the same one
- counts: int32 [32], P(('tiles', 'rows')), may hold values from 4 to 8, as said below
- classes: int32 [256], P(('tiles', 'rows')), may hold values from 0 to 14
- fpn_weight: bfloat16 [2304, 256], replicated, may hold values from -0.125 to 0.125
- head_weight: bfloat16 [2304, 256], replicated, may hold values from -0.125 to 0.125
- deconv_weight: bfloat16 [256, 1024], replicated, may hold values from -0.375 to 0.375
- class_weight: bfloat16 [15, 256], replicated, may hold values from -0.375 to 0.375
Outputs:
- masks: float32 [256, 1024], P(('tiles', 'rows'))
The draws below stay inside these ranges and needn't reach their ends.
Inputs may be any that keep to these rules, and one draw needn't show every extreme that they name: corners[q, 0] lies in owner q // 8's band of rows 16 (q // 8) .. 16 (q // 8 + 1) - 1; corners[q, 1] is at most 496. `offsets`: in each owner's 8 slots no offset occurs more than 2 times, and some offset occurs exactly 2 times. `counts`: some owner has all 8 slots live.
All inputs are finite; a program needn't handle non-finite values.
Results may differ from the reference program's by a relative error of at most 0.0051.
Values may be sent and summed in bfloat16 or wider, within the bound.
A program may use at most 192 MiB of HBM per device.

```python
import math
import jax
import jax.numpy as jnp
import numpy as np
from jax import lax

CHANNELS = 256
CLASSES = 15
ROWS_DEV = 16
COLS = 512
ROI_SIZE = 16
ROI_DEV = 8
WINDOW = 4
SLOTS = 2
MAP_ROWS = 512
ROIS = 256
HEAD_SLOTS = 256
MASK_CELLS = 1024
N_ROWS = 32


def draw_corners(key, part):
    key_rows = jax.random.fold_in(key, 11)
    key_cols = jax.random.fold_in(key, 12)
    owner = jnp.arange(ROIS, dtype=jnp.int32) // ROI_DEV
    rows_in = jax.random.randint(key_rows, (ROIS,), 0, ROWS_DEV, dtype=jnp.int32)
    cols_at = jax.random.randint(key_cols, (ROIS,), 0, COLS - ROI_SIZE + 1, dtype=jnp.int32)
    return jnp.stack([owner * ROWS_DEV + rows_in, cols_at], 1)


def draw_counts(key, part):
    key_counts = jax.random.fold_in(key, 21)
    key_full = jax.random.fold_in(key, 22)
    values = jax.random.randint(key_counts, (N_ROWS,), ROI_DEV // 2, ROI_DEV + 1, dtype=jnp.int32)
    fullest = jax.random.randint(key_full, (), 0, N_ROWS, dtype=jnp.int32)
    return jnp.where(jnp.arange(N_ROWS, dtype=jnp.int32) == fullest, ROI_DEV, values)


def place_ends(entries, own_key, smallest, high):
    extent = entries.shape
    index_at = [jax.random.randint(jax.random.fold_in(own_key, axis), (), 0, extent[axis]) for axis in range(len(extent))]
    entries = entries.at[tuple(index_at)].set(smallest)
    longest = extent.index(max(extent))
    index_at[longest] = (index_at[longest] + 1) % extent[longest]
    return entries.at[tuple(index_at)].set(high)


def levels(key, extent, split, smallest, top_value):
    def one(dim, shards_of):
        steps = jax.random.uniform(jax.random.fold_in(jax.random.fold_in(key, 6), dim), (shards_of,), jnp.float32, smallest / len(split), top_value / len(split))
        return jnp.repeat(jnp.exp(steps), extent[dim] // shards_of).reshape((-1,) + (1,) * (len(extent) - dim - 1))

    factor_of = one(*split[0])
    for cut in split[1:]:
        factor_of = factor_of * one(*cut)
    return factor_of


def shared_out(rng, own, number, rows, number_of, top, bound, skew):
    ranking = jax.random.permutation(rng, number_of)
    crowded, usual = portions_of(number_of, rows * top, bound, skew, True), portions_of(number_of, rows * top, bound, skew, False)
    places = jnp.arange(number_of)

    def named(lengths, offset_by):
        used = int((lengths > 0).sum())
        fixed = max(1, used // 4)
        moved = fixed + (places - fixed + offset_by * (used - fixed)) % max(1, number_of - fixed)
        return jnp.zeros((number_of,), jnp.int32).at[ranking[jnp.where(places < fixed, places, moved)]].set(jnp.asarray(lengths, jnp.int32))

    lengths = jnp.where(number % 4 == 0, named(crowded, number // 4), named(usual, number - number // 4 - 1))
    mixed = jax.random.permutation(jax.random.fold_in(own, 3), number_of)
    giver, receiver = mixed[0:number_of // 2 * 2:2], mixed[1:number_of // 2 * 2:2]
    margin = jnp.minimum(lengths[giver] - 1, bound - lengths[receiver]) // 2
    margin = jnp.where((giver == ranking[0]) | (receiver == ranking[0]) | (lengths[receiver] == 0), 0, jnp.maximum(margin, 0))
    moved = jax.random.randint(jax.random.fold_in(own, 4), (number_of // 2,), 0, 1 << 20) % (margin + 1)
    lengths = lengths.at[giver].add(-moved).at[receiver].add(moved)
    members = jnp.searchsorted(jnp.cumsum(lengths), jnp.arange(rows * top), side="right").astype(jnp.int32)
    listing = members.reshape(top, rows).T
    listing = listing[jax.random.permutation(jax.random.fold_in(own, 1), rows)]
    offset_by = jax.random.randint(jax.random.fold_in(own, 2), (rows, 1), 0, top)
    return jnp.take_along_axis(listing, (jnp.arange(top)[None, :] + offset_by) % top, axis=1)


def portions_of(amount, total, reach, lean, full):
    portions = [(1 << 20) // math.isqrt(standing ** lean) + 1 for standing in range(1, amount + 1)]
    largest = reach if full else min(reach, max(-(-total // amount), total * portions[0] // sum(portions)))
    least = 1 if total - largest >= amount - 1 else 0
    given, rest = [largest] + [least] * (amount - 1), total - largest - least * (amount - 1)
    while rest > 0:
        movable = [i for i in range(1, amount) if given[i] < largest] or [i for i in range(1, amount) if given[i] < reach]
        mass, left = sum([portions[i] for i in movable]), rest
        for i in movable:
            addition = min(reach - given[i], max(1, left * portions[i] // mass), rest)
            given[i] = given[i] + addition
            rest = rest - addition
    return np.array(given)


def scatter_about(rng, shape, scale, bound, cuts=(), kind=jnp.bfloat16):
    level = levels(rng, shape, cuts, -0.22, 0.18) if cuts else 1.0
    entries = jax.random.normal(rng, shape, jnp.float32) * scale * level
    return jnp.minimum(jnp.maximum(entries, -bound), bound).astype(kind)


def setup_inputs(seed: int = 0, part: int = 0) -> dict:
    keys = jax.random.split(jax.random.key(seed), 10)
    part_keys = jax.random.split(jax.random.fold_in(keys[9], part), 10)
    features = scatter_about(part_keys[0], (MAP_ROWS, COLS, CHANNELS), 1.0, 6.0, ((0, 32),))
    corners = draw_corners(jax.random.fold_in(jax.random.fold_in(keys[9], part), 71), part)
    offsets_keys = jax.random.split(jax.random.fold_in(part_keys[2], 1), ROIS // ROI_DEV)
    offsets_turns = jax.random.permutation(jax.random.fold_in(part_keys[2], 3), ROIS // ROI_DEV)
    offsets = jax.vmap(lambda own, number: shared_out(jax.random.fold_in(part_keys[2], 2), own, number, ROI_DEV, WINDOW, 1, SLOTS, 1))(offsets_keys, offsets_turns).reshape((ROIS, 1))
    counts = draw_counts(jax.random.fold_in(jax.random.fold_in(keys[9], part), 71), part)
    classes = place_ends(jax.random.randint(part_keys[4], (ROIS,), 0, CLASSES), jax.random.fold_in(part_keys[4], 1), 0, CLASSES - 1).astype(jnp.int32)
    fpn_weight = scatter_about(keys[5], (9 * CHANNELS, CHANNELS), (9 * CHANNELS) ** -0.5, 0.125)
    head_weight = scatter_about(keys[6], (9 * CHANNELS, CHANNELS), (9 * CHANNELS) ** -0.5, 0.125)
    deconv_weight = scatter_about(keys[7], (CHANNELS, 4 * CHANNELS), CHANNELS ** -0.5, 0.375)
    class_weight = scatter_about(keys[8], (CLASSES, CHANNELS), CHANNELS ** -0.5, 0.375)
    return dict(features=features, corners=corners, offsets=offsets, counts=counts, classes=classes, fpn_weight=fpn_weight, head_weight=head_weight, deconv_weight=deconv_weight, class_weight=class_weight)


def conv_taps(padded, weights):
    chans = padded.shape[-1]
    height = padded.shape[-3] - 2
    width = padded.shape[-2] - 2
    total = jnp.zeros(padded.shape[:-3] + (height, width, weights.shape[1]), jnp.float32)
    for tap in range(9):
        row_off = tap // 3
        col_off = tap % 3
        window = padded[..., row_off:row_off + height, col_off:col_off + width, :].astype(jnp.float32)
        piece = weights[tap * chans:(tap + 1) * chans].astype(jnp.float32)
        total = total + jnp.einsum("...c,cd->...d", window, piece, precision=lax.Precision.HIGHEST)
    return total


def mask_head(blocks, class_ids, head_weight, deconv_weight, class_weight):
    count, side, _, chans = blocks.shape
    padded = jnp.pad(blocks, ((0, 0), (1, 1), (1, 1), (0, 0)))
    hidden = jax.nn.relu(conv_taps(padded, head_weight)).astype(jnp.bfloat16)
    upsampled = jnp.einsum("bhwc,ck->bhwk", hidden.astype(jnp.float32), deconv_weight.astype(jnp.float32), precision=lax.Precision.HIGHEST)
    upsampled = jax.nn.relu(upsampled).astype(jnp.bfloat16).reshape(count, side, side, 2, 2, chans)
    chosen = class_weight[class_ids].astype(jnp.float32)
    logit = jnp.einsum("bhwyxc,bc->bhwyx", upsampled.astype(jnp.float32), chosen, precision=lax.Precision.HIGHEST)
    return logit.transpose(0, 1, 3, 2, 4).reshape(count, 4 * side * side)


def reference(features, corners, offsets, counts, classes, fpn_weight, head_weight, deconv_weight, class_weight):
    padded = jnp.pad(features, ((1, 1), (1, 1), (0, 0)))
    pyramid = conv_taps(padded, fpn_weight).astype(jnp.bfloat16)
    extended = jnp.concatenate([pyramid, jnp.zeros((ROI_SIZE - 1, COLS, CHANNELS), jnp.bfloat16)], 0)

    def crop(row_at, col_at):
        return lax.dynamic_slice(extended, (row_at, col_at, jnp.int32(0)), (ROI_SIZE, ROI_SIZE, CHANNELS))

    def per_owner(args):
        tops, lefts, class_ids = args
        blocks = jax.vmap(crop)(tops, lefts)
        return mask_head(blocks, class_ids, head_weight, deconv_weight, class_weight)

    logits = lax.map(per_owner, (corners[:, 0].astype(jnp.int32).reshape(N_ROWS, ROI_DEV),
                                 corners[:, 1].astype(jnp.int32).reshape(N_ROWS, ROI_DEV),
                                 classes.reshape(N_ROWS, ROI_DEV)))
    logits = logits.reshape(ROIS, MASK_CELLS)
    ordinal = jnp.arange(ROIS, dtype=jnp.int32)
    owner = ordinal // ROI_DEV
    local = ordinal % ROI_DEV
    valid = local < counts[owner]
    target = offsets[:, 0].astype(jnp.int32)
    target2 = target.reshape(N_ROWS, ROI_DEV)
    valid2 = valid.reshape(N_ROWS, ROI_DEV)
    slot_ids = jnp.arange(ROI_DEV, dtype=jnp.int32)
    earlier = (target2[:, :, None] == target2[:, None, :]) & valid2[:, None, :] & (slot_ids[None, :] < slot_ids[:, None])[None]
    rank = jnp.sum(earlier.astype(jnp.int32), -1).reshape(ROIS)
    head = (owner + target) % N_ROWS
    row_of = jnp.where(valid, head * (WINDOW * SLOTS) + target * SLOTS + rank, HEAD_SLOTS).astype(jnp.int32)
    masks = jnp.zeros((HEAD_SLOTS, MASK_CELLS), jnp.float32).at[row_of].set(logits, mode="drop")
    return masks
```

```python
import functools

import jax
import jax.numpy as jnp
from jax import lax
from jax.experimental import pallas as pl
from jax.experimental.pallas import tpu as pltpu
from jax.sharding import PartitionSpec as P

SIDE = 16
CELLS = SIDE * SIDE
WINDOW = 4
SLOTS = 2
EDGE = 16
GROUP = 2
CHUNKS = 4
MESH = pl.DeviceIdType.MESH
BF16, F32 = jnp.bfloat16, jnp.float32


def order_of(offsets, order, rois):
    held = [offsets[0, q] for q in range(rois)]
    place = []
    for q in range(rois):
        rank = jnp.int32(0)
        for p in range(q):
            rank = rank + (held[p] == held[q]).astype(jnp.int32)
        place.append((WINDOW - 1 - held[q]) * SLOTS + rank)
    for p in range(rois):
        slot = jnp.int32(0)
        for q in range(1, rois):
            slot = jnp.where(place[q] == p, q, slot)
        order[p] = slot


def kernel(
    count,
    corners_sm,
    corners_vm,
    offset_sm,
    offset_vm,
    count_sm,
    class_sm,
    feat,
    fpn_hbm,
    head_hbm,
    dec_hbm,
    cls_w,
    out,
    band,
    wide,
    fpn_w,
    head_w,
    dec_w,
    dec_t,
    near_vm,
    near_off_vm,
    near_sm,
    near_off_sm,
    order,
    near_order,
    sent,
    got,
    row_sent,
    row_got,
    ends,
    joined,
    wins,
    blocks,
    shifted,
    hidden,
    outgoing,
    incoming,
    load_sem,
    small_send,
    small_recv,
    piece_send,
    piece_recv,
    mask_send,
    mask_recv,
    ready,
):
    me = lax.axis_index("rows")
    rois = sent.shape[0]
    band_rows, columns, chans = band.shape
    halves, lanes = wide.shape[0], wide.shape[-1]
    has_up = me > 0
    has_down = me < count - 1

    def at(step):
        return {"rows": lax.rem(me + step + count, count)}

    barrier = pltpu.get_barrier_semaphore()
    for step in (1, -1):
        pl.semaphore_signal(barrier, inc=1, device_id=at(step), device_id_type=MESH)

    chunk = band_rows // CHUNKS
    band_loads = [
        pltpu.make_async_copy(
            feat.at[pl.ds(c * chunk, chunk)], band.at[pl.ds(c * chunk, chunk)], load_sem.at[c]
        )
        for c in range(CHUNKS)
    ]
    loads = [
        pltpu.make_async_copy(fpn_hbm, fpn_w, load_sem.at[CHUNKS]),
        pltpu.make_async_copy(head_hbm, head_w, load_sem.at[CHUNKS + 1]),
        pltpu.make_async_copy(dec_hbm, dec_w, load_sem.at[CHUNKS + 2]),
    ]
    for load in band_loads + loads:
        load.start()

    pl.semaphore_wait(barrier, 2)

    def small(k, src, dst):
        side = k // 2
        return pltpu.make_async_remote_copy(
            src_ref=src,
            dst_ref=dst.at[side],
            send_sem=small_send.at[k],
            recv_sem=small_recv.at[k],
            device_id=at(1 if side == 0 else -1),
            device_id_type=MESH,
        )

    smalls = [
        small(0, corners_vm, near_vm),
        small(1, offset_vm, near_off_vm),
        small(2, corners_vm, near_vm),
        small(3, offset_vm, near_off_vm),
    ]

    @pl.when(has_down)
    def _():
        smalls[0].start()
        smalls[1].start()

    @pl.when(has_up)
    def _():
        smalls[2].start()
        smalls[3].start()

    pl.semaphore_signal(ready.at[0], inc=1, device_id=at(-1), device_id_type=MESH)

    wide[:, :, 0:EDGE, :] = jnp.zeros((halves, band_rows, EDGE, lanes), F32)
    wide[:, :, EDGE + columns :, :] = jnp.zeros((halves, band_rows, EDGE, lanes), F32)

    for c in range(CHUNKS):
        band_loads[c].wait()

        def widen(i, carry):
            for h in range(halves):
                wide[h, pl.ds(i, 1), EDGE : EDGE + columns, :] = band[
                    pl.ds(i, 1), :, h * lanes : (h + 1) * lanes
                ].astype(F32)
            return carry

        lax.fori_loop(c * chunk, (c + 1) * chunk, widen, 0)

    def piece(p):
        return pltpu.make_async_remote_copy(
            src_ref=sent.at[p],
            dst_ref=got.at[p],
            send_sem=piece_send.at[p],
            recv_sem=piece_recv.at[p],
            device_id=at(-1),
            device_id_type=MESH,
        )

    row_copy = pltpu.make_async_remote_copy(
        src_ref=row_sent,
        dst_ref=row_got,
        send_sem=small_send.at[4],
        recv_sem=small_recv.at[4],
        device_id=at(1),
        device_id_type=MESH,
    )

    def near_in(side):
        first = 2 * side
        smalls[first].wait_recv()
        smalls[first + 1].wait_recv()
        moves = [
            pltpu.make_async_copy(near_vm.at[side], near_sm.at[side], load_sem.at[CHUNKS + 3]),
            pltpu.make_async_copy(
                near_off_vm.at[side], near_off_sm.at[side], load_sem.at[CHUNKS + 4]
            ),
        ]
        for move in moves:
            move.start()
        for move in moves:
            move.wait()
        order_of(near_off_sm.at[side], near_order.at[side], rois)

    @pl.when(has_down)
    def _():
        near_in(1)
        for p in range(rois):
            start = near_sm[1, 1, near_order[1, p]] + (EDGE - 1)
            for h in range(halves):
                part = slice(h * lanes, (h + 1) * lanes)
                row_sent[p, :, part] = wide[
                    h, band_rows - 1, pl.ds(start + 1, SIDE), :
                ].astype(BF16)
                ends[0, p : p + 1, part] = wide[h, band_rows - 1, pl.ds(start, 1), :]
                ends[0, rois + p : rois + p + 1, part] = wide[
                    h, band_rows - 1, pl.ds(start + SIDE + 1, 1), :
                ]
        row_sent[rois] = ends[0].astype(BF16)
        row_copy.start()

    @pl.when(has_up)
    def _():
        near_in(0)

        def gather(p, carry):
            start = near_sm[0, 1, near_order[0, p]] + (EDGE - 1)
            for h in range(halves):
                part = slice(h * lanes, (h + 1) * lanes)
                for i in range(band_rows):
                    sent[p, i, :, part] = wide[h, i, pl.ds(start + 1, SIDE), :].astype(BF16)
                    ends[0, i : i + 1, part] = wide[h, i, pl.ds(start, 1), :]
                    ends[1, i : i + 1, part] = wide[h, i, pl.ds(start + SIDE + 1, 1), :]
            sent[p, SIDE:] = ends[...].astype(BF16)
            piece(p).start()
            return carry

        lax.fori_loop(0, rois, gather, 0)

    order_of(offset_sm, order, rois)

    def own(p, carry):
        start = corners_sm[1, order[p]] + (EDGE - 1)
        for dj in range(3):
            for h in range(halves):
                for i in range(band_rows):
                    wins[p, dj, i + 1, :, h * lanes : (h + 1) * lanes] = wide[
                        h, i, pl.ds(start + dj, SIDE), :
                    ].astype(BF16)
        return carry

    lax.fori_loop(0, rois, own, 0)

    blocks[...] = jnp.zeros_like(blocks)
    for u in range(GROUP):
        for dj in range(3):
            shifted[dj, u, 0] = jnp.zeros((SIDE, chans), BF16)
            shifted[dj, u, SIDE + 1] = jnp.zeros((SIDE, chans), BF16)

    @pl.when(jnp.logical_not(has_down))
    def _():
        got[...] = jnp.zeros_like(got)

    for load in loads:
        load.wait()
    for yx in range(4):
        dec_t[yx * chans : (yx + 1) * chans] = jnp.transpose(
            dec_w[:, yx * chans : (yx + 1) * chans]
        )

    @pl.when(has_up)
    def _():
        row_copy.wait_recv()

    @pl.when(jnp.logical_not(has_up))
    def _():
        row_got[...] = jnp.zeros_like(row_got)

    joined[0:rois, 8 : 8 + SIDE, :] = row_got[0:rois].astype(F32)
    ends[0] = row_got[rois].astype(F32)
    for p in range(rois):
        joined[p, 7:8, :] = ends[0, p : p + 1, :]
        joined[p, 8 + SIDE : 9 + SIDE, :] = ends[0, rois + p : rois + p + 1, :]
    for dj in range(3):
        wins[:, dj, 0] = joined[0:rois, 7 + dj : 7 + dj + SIDE, :].astype(BF16)

    limit = jnp.where(has_down, 2 * band_rows, band_rows)

    pl.semaphore_wait(ready.at[0], 1)
    pl.semaphore_signal(ready.at[1], inc=1, device_id=at(-1), device_id_type=MESH)

    def mask(f):
        return pltpu.make_async_remote_copy(
            src_ref=outgoing.at[f],
            dst_ref=incoming.at[f],
            send_sem=mask_send.at[f],
            recv_sem=mask_recv.at[f],
            device_id=at(f),
            device_id_type=MESH,
        )

    def join(p, carry):
        @pl.when(has_down)
        def _():
            piece(p).wait_recv()

        joined[:, 8 : 8 + SIDE, :] = got[p, 0:SIDE].astype(F32)
        ends[...] = got[p, SIDE:].astype(F32)
        for i in range(band_rows):
            joined[i, 7:8, :] = ends[0, i : i + 1, :]
            joined[i, 8 + SIDE : 9 + SIDE, :] = ends[1, i : i + 1, :]
        wins[p, 0, band_rows + 1 :] = joined[:, 7 : 7 + SIDE, :].astype(BF16)
        wins[p, 1, band_rows + 1 :] = got[p, 0:SIDE]
        wins[p, 2, band_rows + 1 :] = joined[:, 9 : 9 + SIDE, :].astype(BF16)
        return carry

    def fpn(g, carry):
        base = g * GROUP
        tops = [lax.rem(corners_sm[0, order[base + u]], band_rows) for u in range(GROUP)]
        lhs = jnp.concatenate(
            [
                jnp.concatenate(
                    [
                        wins[base + u, tap % 3, pl.ds(tops[u] + tap // 3, SIDE)].reshape(
                            CELLS, chans
                        )
                        for u in range(GROUP)
                    ],
                    axis=0,
                )
                for tap in range(9)
            ],
            axis=1,
        )
        total = jnp.dot(lhs, fpn_w[...], preferred_element_type=F32)
        total = total.reshape(GROUP, SIDE, SIDE, chans)
        row = lax.broadcasted_iota(jnp.int32, (SIDE, SIDE, chans), 0)
        for u in range(GROUP):
            kept = jnp.where(row + tops[u] < limit, total[u], 0.0)
            blocks[u, :, 8 : 8 + SIDE, :] = kept
            shifted[1, u, 1 : 1 + SIDE] = kept.astype(BF16)
        for u in range(GROUP):
            for dj in (0, 2):
                shifted[dj, u, 1 : 1 + SIDE] = blocks[u, :, 7 + dj : 7 + dj + SIDE, :].astype(BF16)
        return carry

    def head(g, carry):
        lhs = jnp.concatenate(
            [
                shifted[tap % 3, :, tap // 3 : tap // 3 + SIDE].reshape(GROUP * CELLS, chans)
                for tap in range(9)
            ],
            axis=1,
        )
        total = jnp.dot(lhs, head_w[...], preferred_element_type=F32)
        hidden[...] = jnp.maximum(total, 0.0).astype(BF16)
        return carry

    def tail(g, carry):
        base = g * GROUP
        for u in range(GROUP):
            slot = order[base + u]
            rows = cls_w[...].astype(F32)
            which = lax.broadcasted_iota(jnp.int32, rows.shape, 0)
            chosen = jnp.sum(
                jnp.where(which == class_sm[slot], rows, 0.0), axis=0, keepdims=True
            )
            column = jnp.transpose(jnp.broadcast_to(chosen, (lanes, chans)))
            live = slot < count_sm[0]
            for yx in range(4):
                up = lax.dot_general(
                    dec_t[yx * chans : (yx + 1) * chans],
                    hidden[u * CELLS : (u + 1) * CELLS],
                    (((1,), (1,)), ((), ())),
                    preferred_element_type=F32,
                )
                up = jnp.maximum(up, 0.0).astype(BF16).astype(F32)
                for v in range(CELLS // lanes):
                    part = slice(v * lanes, (v + 1) * lanes)
                    logit = jnp.sum(up[:, part] * column, axis=0, keepdims=True)
                    outgoing[WINDOW - 1 - g, u, yx : yx + 1, part] = jnp.where(live, logit, 0.0)
        return carry

    pl.semaphore_wait(ready.at[1], 1)

    def group(g, carry):
        lax.fori_loop(g * GROUP, (g + 1) * GROUP, join, 0)
        lax.fori_loop(g, g + 1, fpn, 0)
        lax.fori_loop(g, g + 1, head, 0)
        lax.fori_loop(g, g + 1, tail, 0)

        @pl.when(g < WINDOW - 1)
        def _():
            mask(WINDOW - 1 - g).start()

        return carry

    lax.fori_loop(0, rois // GROUP, group, 0)

    out[0:SLOTS] = outgoing[0]
    for f in range(1, WINDOW):
        mask(f).wait_recv()
        out[f * SLOTS : (f + 1) * SLOTS] = incoming[f]

    for f in range(1, WINDOW):
        mask(f).wait_send()

    @pl.when(has_down)
    def _():
        smalls[0].wait_send()
        smalls[1].wait_send()
        row_copy.wait_send()

    @pl.when(has_up)
    def _():
        smalls[2].wait_send()
        smalls[3].wait_send()

        def drain(p, carry):
            piece(p).wait_send()
            return carry

        lax.fori_loop(0, rois, drain, 0)


def body(
    count,
    features,
    corners,
    offsets,
    counts,
    classes,
    fpn_weight,
    head_weight,
    deconv_weight,
    class_weight,
):
    band_rows, columns, chans = features.shape
    rois = corners.shape[0]
    spots = corners.T
    turns = offsets.T
    smem = pl.BlockSpec(memory_space=pltpu.SMEM)
    vmem = pl.BlockSpec(memory_space=pltpu.VMEM)
    anyw = pl.BlockSpec(memory_space=pl.ANY)
    masks = pl.pallas_call(
        functools.partial(kernel, count),
        out_shape=jax.ShapeDtypeStruct((WINDOW * SLOTS, 4, CELLS), F32),
        in_specs=[smem, vmem, smem, vmem, smem, smem, anyw, anyw, anyw, anyw, vmem],
        out_specs=vmem,
        scratch_shapes=[
            pltpu.VMEM(features.shape, BF16),
            pltpu.VMEM((chans // 128, band_rows, columns + 2 * EDGE, 128), F32),
            pltpu.VMEM(fpn_weight.shape, BF16),
            pltpu.VMEM(head_weight.shape, BF16),
            pltpu.VMEM(deconv_weight.shape, BF16),
            pltpu.VMEM(deconv_weight.shape[::-1], BF16),
            pltpu.VMEM((2,) + spots.shape, jnp.int32),
            pltpu.VMEM((2,) + turns.shape, jnp.int32),
            pltpu.SMEM((2,) + spots.shape, jnp.int32),
            pltpu.SMEM((2,) + turns.shape, jnp.int32),
            pltpu.SMEM((rois,), jnp.int32),
            pltpu.SMEM((2, rois), jnp.int32),
            pltpu.VMEM((rois, SIDE + 2, SIDE, chans), BF16),
            pltpu.VMEM((rois, SIDE + 2, SIDE, chans), BF16),
            pltpu.VMEM((rois + 1, SIDE, chans), BF16),
            pltpu.VMEM((rois + 1, SIDE, chans), BF16),
            pltpu.VMEM((2, SIDE, chans), F32),
            pltpu.VMEM((SIDE, 2 * SIDE, chans), F32),
            pltpu.VMEM((rois, 3, 2 * band_rows + 1, SIDE, chans), BF16),
            pltpu.VMEM((GROUP, SIDE, 2 * SIDE, chans), F32),
            pltpu.VMEM((3, GROUP, SIDE + 2, SIDE, chans), BF16),
            pltpu.VMEM((GROUP * CELLS, chans), BF16),
            pltpu.VMEM((WINDOW, SLOTS, 4, CELLS), F32),
            pltpu.VMEM((WINDOW, SLOTS, 4, CELLS), F32),
            pltpu.SemaphoreType.DMA((CHUNKS + 5,)),
            pltpu.SemaphoreType.DMA((5,)),
            pltpu.SemaphoreType.DMA((5,)),
            pltpu.SemaphoreType.DMA((rois,)),
            pltpu.SemaphoreType.DMA((rois,)),
            pltpu.SemaphoreType.DMA((WINDOW,)),
            pltpu.SemaphoreType.DMA((WINDOW,)),
            pltpu.SemaphoreType.REGULAR((2,)),
        ],
        compiler_params=pltpu.CompilerParams(
            collective_id=0, has_side_effects=True, vmem_limit_bytes=60 * 1024 * 1024
        ),
    )(
        spots,
        spots,
        turns,
        turns,
        counts,
        classes,
        features,
        fpn_weight,
        head_weight,
        deconv_weight,
        class_weight,
    )
    masks = masks.reshape(WINDOW * SLOTS, 2, 2, SIDE, SIDE)
    return masks.transpose(0, 3, 1, 4, 2).reshape(WINDOW * SLOTS, 4 * CELLS)


def solution(mesh):
    placed = (
        P(("tiles", "rows"), None, None),
        P(("tiles", "rows"), None),
        P(("tiles", "rows"), None),
        P(("tiles", "rows")),
        P(("tiles", "rows")),
        P(),
        P(),
        P(),
        P(),
    )
    return jax.shard_map(
        functools.partial(body, mesh.shape["rows"]),
        mesh=mesh,
        in_specs=placed,
        out_specs=P(("tiles", "rows"), None),
        check_vma=False,
    )
```

```python
import functools

import jax
import jax.numpy as jnp
from jax import lax
from jax.experimental import pallas as pl
from jax.experimental.pallas import tpu as pltpu
from jax.sharding import PartitionSpec as P

SIDE = 16
CELLS = SIDE * SIDE
WINDOW = 4
SLOTS = 2
EDGE = 16
GROUP = 2
CHUNKS = 4
MESH = pl.DeviceIdType.MESH
BF16, F32 = jnp.bfloat16, jnp.float32


def order_of(offsets, corners, order, cols, rois):
    held = [offsets[0, q] for q in range(rois)]
    place = []
    for q in range(rois):
        rank = jnp.int32(0)
        for p in range(q):
            rank = rank + (held[p] == held[q]).astype(jnp.int32)
        place.append((WINDOW - 1 - held[q]) * SLOTS + rank)
    for p in range(rois):
        slot = jnp.int32(0)
        for q in range(1, rois):
            slot = jnp.where(place[q] == p, q, slot)
        order[p] = slot
        cols[0, p] = corners[1, slot]


def kernel(
    count,
    corners_sm,
    offset_sm,
    count_hbm,
    class_sm,
    feat,
    fpn_hbm,
    head_hbm,
    dec_hbm,
    cls_w,
    out,
    band,
    wide,
    fpn_w,
    head_w,
    dec_w,
    dec_t,
    count_sm,
    order,
    cols,
    near_cols,
    below_row,
    sent,
    got,
    row_sent,
    row_got,
    ends,
    joined,
    wins,
    blocks,
    shifted,
    hidden,
    logits,
    outgoing,
    incoming,
    load_sem,
    small_send,
    small_recv,
    piece_send,
    piece_recv,
    mask_send,
    mask_recv,
    ready,
):
    me = lax.axis_index("rows")
    rois = sent.shape[0]
    band_rows, columns, chans = band.shape
    rest = band_rows - 1
    halves, lanes = wide.shape[0], wide.shape[-1]
    has_up = me > 0
    has_down = me < count - 1

    def at(step):
        return {"rows": lax.rem(me + step + count, count)}

    barrier = pltpu.get_barrier_semaphore()
    for step in (1, -1):
        pl.semaphore_signal(barrier, inc=1, device_id=at(step), device_id_type=MESH)

    chunk = band_rows // CHUNKS
    band_loads = [
        pltpu.make_async_copy(
            feat.at[pl.ds(c * chunk, chunk)], band.at[pl.ds(c * chunk, chunk)], load_sem.at[c]
        )
        for c in range(CHUNKS)
    ]
    loads = [
        pltpu.make_async_copy(fpn_hbm, fpn_w, load_sem.at[CHUNKS]),
        pltpu.make_async_copy(head_hbm, head_w, load_sem.at[CHUNKS + 1]),
        pltpu.make_async_copy(dec_hbm, dec_w, load_sem.at[CHUNKS + 2]),
        pltpu.make_async_copy(count_hbm, count_sm, load_sem.at[CHUNKS + 3]),
    ]
    for load in band_loads + loads:
        load.start()

    order_of(offset_sm, corners_sm, order, cols, rois)
    pl.semaphore_wait(barrier, 2)

    first_row = pltpu.make_async_remote_copy(
        src_ref=feat.at[pl.ds(0, 1)],
        dst_ref=below_row,
        send_sem=small_send.at[3],
        recv_sem=small_recv.at[3],
        device_id=at(-1),
        device_id_type=MESH,
    )

    smalls = [
        pltpu.make_async_remote_copy(
            src_ref=cols,
            dst_ref=near_cols.at[side],
            send_sem=small_send.at[side],
            recv_sem=small_recv.at[side],
            device_id=at(1 - 2 * side),
            device_id_type=MESH,
        )
        for side in range(2)
    ]

    @pl.when(has_down)
    def _():
        smalls[0].start()

    @pl.when(has_up)
    def _():
        smalls[1].start()
        first_row.start()

    pl.semaphore_signal(ready.at[0], inc=1, device_id=at(-1), device_id_type=MESH)

    wide[:, :, 0:EDGE, :] = jnp.zeros((halves, band_rows + 1, EDGE, lanes), F32)
    wide[:, :, EDGE + columns :, :] = jnp.zeros((halves, band_rows + 1, EDGE, lanes), F32)

    for c in range(CHUNKS):
        band_loads[c].wait()

        def widen(i, carry):
            for h in range(halves):
                wide[h, pl.ds(i, 1), EDGE : EDGE + columns, :] = band[
                    pl.ds(i, 1), :, h * lanes : (h + 1) * lanes
                ].astype(F32)
            return carry

        lax.fori_loop(c * chunk, (c + 1) * chunk, widen, 0)

    def piece(p):
        return pltpu.make_async_remote_copy(
            src_ref=sent.at[p],
            dst_ref=got.at[p],
            send_sem=piece_send.at[p],
            recv_sem=piece_recv.at[p],
            device_id=at(-1),
            device_id_type=MESH,
        )

    row_copy = pltpu.make_async_remote_copy(
        src_ref=row_sent,
        dst_ref=row_got,
        send_sem=small_send.at[2],
        recv_sem=small_recv.at[2],
        device_id=at(1),
        device_id_type=MESH,
    )

    @pl.when(has_down)
    def _():
        smalls[1].wait_recv()
        for p in range(rois):
            start = near_cols[1, 0, p] + (EDGE - 1)
            for h in range(halves):
                part = slice(h * lanes, (h + 1) * lanes)
                row_sent[p, :, part] = wide[
                    h, band_rows - 1, pl.ds(start + 1, SIDE), :
                ].astype(BF16)
                ends[0, p : p + 1, part] = wide[h, band_rows - 1, pl.ds(start, 1), :]
                ends[0, rois + p : rois + p + 1, part] = wide[
                    h, band_rows - 1, pl.ds(start + SIDE + 1, 1), :
                ]
        row_sent[rois] = ends[0].astype(BF16)
        row_copy.start()

    @pl.when(has_up)
    def _():
        smalls[0].wait_recv()

        def gather(p, carry):
            start = near_cols[0, 0, p] + (EDGE - 1)
            for h in range(halves):
                part = slice(h * lanes, (h + 1) * lanes)
                for i in range(rest):
                    sent[p, i, :, part] = wide[h, i + 1, pl.ds(start + 1, SIDE), :].astype(BF16)
                    ends[0, i : i + 1, part] = wide[h, i + 1, pl.ds(start, 1), :]
                    ends[1, i : i + 1, part] = wide[h, i + 1, pl.ds(start + SIDE + 1, 1), :]
            sent[p, rest:] = ends[...].astype(BF16)
            piece(p).start()
            return carry

        lax.fori_loop(0, rois, gather, 0)

    pl.semaphore_wait(ready.at[0], 1)
    pl.semaphore_signal(ready.at[1], inc=1, device_id=at(-1), device_id_type=MESH)

    @pl.when(has_down)
    def _():
        first_row.wait_recv()

    @pl.when(jnp.logical_not(has_down))
    def _():
        below_row[...] = jnp.zeros_like(below_row)

    for h in range(halves):
        wide[h, band_rows :, EDGE : EDGE + columns, :] = below_row[
            :, :, h * lanes : (h + 1) * lanes
        ].astype(F32)

    def own(p, carry):
        start = cols[0, p] + (EDGE - 1)
        for dj in range(3):
            for h in range(halves):
                for i in range(band_rows + 1):
                    wins[p, dj, i + 1, :, h * lanes : (h + 1) * lanes] = wide[
                        h, i, pl.ds(start + dj, SIDE), :
                    ].astype(BF16)
        return carry

    lax.fori_loop(0, rois, own, 0)

    blocks[...] = jnp.zeros_like(blocks)
    for u in range(GROUP):
        for dj in range(3):
            shifted[dj, u, 0] = jnp.zeros((SIDE, chans), BF16)
            shifted[dj, u, SIDE + 1] = jnp.zeros((SIDE, chans), BF16)

    @pl.when(jnp.logical_not(has_down))
    def _():
        got[...] = jnp.zeros_like(got)

    for load in loads:
        load.wait()
    for yx in range(4):
        dec_t[yx * chans : (yx + 1) * chans] = jnp.transpose(
            dec_w[:, yx * chans : (yx + 1) * chans]
        )

    @pl.when(has_up)
    def _():
        row_copy.wait_recv()

    @pl.when(jnp.logical_not(has_up))
    def _():
        row_got[...] = jnp.zeros_like(row_got)

    joined[0:rois, 8 : 8 + SIDE, :] = row_got[0:rois].astype(F32)
    ends[0] = row_got[rois].astype(F32)
    for p in range(rois):
        joined[p, 7:8, :] = ends[0, p : p + 1, :]
        joined[p, 8 + SIDE : 9 + SIDE, :] = ends[0, rois + p : rois + p + 1, :]
    for dj in range(3):
        wins[:, dj, 0] = joined[0:rois, 7 + dj : 7 + dj + SIDE, :].astype(BF16)

    limit = jnp.where(has_down, 2 * band_rows, band_rows)

    def mask(f):
        return pltpu.make_async_remote_copy(
            src_ref=outgoing.at[f],
            dst_ref=incoming.at[f],
            send_sem=mask_send.at[f],
            recv_sem=mask_recv.at[f],
            device_id=at(f),
            device_id_type=MESH,
        )

    def join(p, carry):
        @pl.when(has_down)
        def _():
            piece(p).wait_recv()

        joined[0:rest, 8 : 8 + SIDE, :] = got[p, 0:rest].astype(F32)
        ends[...] = got[p, rest:].astype(F32)
        for i in range(rest):
            joined[i, 7:8, :] = ends[0, i : i + 1, :]
            joined[i, 8 + SIDE : 9 + SIDE, :] = ends[1, i : i + 1, :]
        wins[p, 0, band_rows + 2 :] = joined[0:rest, 7 : 7 + SIDE, :].astype(BF16)
        wins[p, 1, band_rows + 2 :] = got[p, 0:rest]
        wins[p, 2, band_rows + 2 :] = joined[0:rest, 9 : 9 + SIDE, :].astype(BF16)
        return carry

    def fpn(size, base, carry):
        tops = [lax.rem(corners_sm[0, order[base + u]], band_rows) for u in range(size)]
        lhs = jnp.concatenate(
            [
                jnp.concatenate(
                    [
                        wins[base + u, tap % 3, pl.ds(tops[u] + tap // 3, SIDE)].reshape(
                            CELLS, chans
                        )
                        for u in range(size)
                    ],
                    axis=0,
                )
                for tap in range(9)
            ],
            axis=1,
        )
        total = jnp.dot(lhs, fpn_w[...], preferred_element_type=F32)
        total = total.reshape(size, SIDE, SIDE, chans)
        row = lax.broadcasted_iota(jnp.int32, (SIDE, SIDE, chans), 0)
        for u in range(size):
            kept = jnp.where(row + tops[u] < limit, total[u], 0.0)
            blocks[u, :, 8 : 8 + SIDE, :] = kept
            shifted[1, u, 1 : 1 + SIDE] = kept.astype(BF16)
        for u in range(size):
            for dj in (0, 2):
                shifted[dj, u, 1 : 1 + SIDE] = blocks[u, :, 7 + dj : 7 + dj + SIDE, :].astype(BF16)
        return carry

    def head(size, base, carry):
        lhs = jnp.concatenate(
            [
                shifted[tap % 3, 0:size, tap // 3 : tap // 3 + SIDE].reshape(size * CELLS, chans)
                for tap in range(9)
            ],
            axis=1,
        )
        total = jnp.dot(lhs, head_w[...], preferred_element_type=F32)
        hidden[0 : size * CELLS] = jnp.maximum(total, 0.0).astype(BF16)
        return carry

    def tail(size, base, carry):
        for u in range(size):
            slot = order[base + u]
            rows = cls_w[...].astype(F32)
            which = lax.broadcasted_iota(jnp.int32, rows.shape, 0)
            chosen = jnp.sum(
                jnp.where(which == class_sm[slot], rows, 0.0), axis=0, keepdims=True
            )
            column = jnp.transpose(jnp.broadcast_to(chosen, (lanes, chans)))
            live = slot < count_sm[0]
            for yx in range(4):
                up = lax.dot_general(
                    dec_t[yx * chans : (yx + 1) * chans],
                    hidden[u * CELLS : (u + 1) * CELLS],
                    (((1,), (1,)), ((), ())),
                    preferred_element_type=F32,
                )
                up = jnp.maximum(up, 0.0).astype(BF16).astype(F32)
                for v in range(CELLS // lanes):
                    part = slice(v * lanes, (v + 1) * lanes)
                    logit = jnp.sum(up[:, part] * column, axis=0, keepdims=True)
                    logits[base + u, yx : yx + 1, part] = jnp.where(live, logit, 0.0)
        return carry

    def spread(g):
        shape = (4 * SLOTS, lanes)
        lane = lax.broadcasted_iota(jnp.int32, shape, 1)
        held = lax.broadcasted_iota(jnp.int32, shape, 0) % 4
        mine = (lane // (2 * SIDE)) % 2 * 2 + lane % 2 == held
        span = lanes // (4 * SIDE)
        pair = logits[pl.ds(g * SLOTS, SLOTS)].reshape(4 * SLOTS, CELLS)
        for k in range(4 * CELLS // lanes):
            v, first = divmod(k * span * SIDE, lanes)
            index = first + lane // (4 * SIDE) * SIDE + lane % (2 * SIDE) // 2
            picked = jnp.take_along_axis(
                pair[:, v * lanes : (v + 1) * lanes], index, axis=1, mode="promise_in_bounds"
            )
            picked = jnp.where(mine, picked, 0.0).reshape(SLOTS, 4, lanes)
            outgoing[WINDOW - 1 - g, :, k * lanes : (k + 1) * lanes] = jnp.sum(picked, axis=1)

    def stages(size, base):
        for stage in (fpn, head, tail):
            lax.fori_loop(base, base + 1, functools.partial(stage, size), 0)

    def group(g, carry):
        lax.fori_loop(g * GROUP, (g + 1) * GROUP, join, 0)
        stages(GROUP, g * GROUP)
        spread(g)

        @pl.when(g == 0)
        def _():
            pl.semaphore_wait(ready.at[1], 1)

        mask(WINDOW - 1 - g).start()
        return carry

    lax.fori_loop(0, WINDOW - 1, group, 0)

    def single(p, carry):
        join(p, carry)
        stages(1, p)
        return carry

    lax.fori_loop(rois - SLOTS, rois, single, 0)
    spread(WINDOW - 1)

    out[0:SLOTS] = outgoing[0]
    for f in range(1, WINDOW):
        mask(f).wait_recv()
        out[f * SLOTS : (f + 1) * SLOTS] = incoming[f]

    for f in range(1, WINDOW):
        mask(f).wait_send()

    @pl.when(has_down)
    def _():
        smalls[0].wait_send()
        row_copy.wait_send()

    @pl.when(has_up)
    def _():
        first_row.wait_send()
        smalls[1].wait_send()

        def drain(p, carry):
            piece(p).wait_send()
            return carry

        lax.fori_loop(0, rois, drain, 0)


def body(
    count,
    features,
    corners,
    offsets,
    counts,
    classes,
    fpn_weight,
    head_weight,
    deconv_weight,
    class_weight,
):
    band_rows, columns, chans = features.shape
    rois = corners.shape[0]
    spots = corners.T
    turns = offsets.T
    smem = pl.BlockSpec(memory_space=pltpu.SMEM)
    vmem = pl.BlockSpec(memory_space=pltpu.VMEM)
    anyw = pl.BlockSpec(memory_space=pl.ANY)
    hbm = pl.BlockSpec(memory_space=pltpu.HBM)
    return pl.pallas_call(
        functools.partial(kernel, count),
        out_shape=jax.ShapeDtypeStruct((WINDOW * SLOTS, 4 * CELLS), F32),
        in_specs=[smem, smem, hbm, smem, anyw, anyw, anyw, anyw, vmem],
        out_specs=vmem,
        scratch_shapes=[
            pltpu.VMEM(features.shape, BF16),
            pltpu.VMEM((chans // 128, band_rows + 1, columns + 2 * EDGE, 128), F32),
            pltpu.VMEM(fpn_weight.shape, BF16),
            pltpu.VMEM(head_weight.shape, BF16),
            pltpu.VMEM(deconv_weight.shape, BF16),
            pltpu.VMEM(deconv_weight.shape[::-1], BF16),
            pltpu.SMEM((1,), jnp.int32),
            pltpu.SMEM((rois,), jnp.int32),
            pltpu.SMEM(turns.shape, jnp.int32),
            pltpu.SMEM((2,) + turns.shape, jnp.int32),
            pltpu.VMEM((1, columns, chans), BF16),
            pltpu.VMEM((rois, band_rows + 1, SIDE, chans), BF16),
            pltpu.VMEM((rois, band_rows + 1, SIDE, chans), BF16),
            pltpu.VMEM((rois + 1, SIDE, chans), BF16),
            pltpu.VMEM((rois + 1, SIDE, chans), BF16),
            pltpu.VMEM((2, SIDE, chans), F32),
            pltpu.VMEM((SIDE, 2 * SIDE, chans), F32),
            pltpu.VMEM((rois, 3, 2 * band_rows + 1, SIDE, chans), BF16),
            pltpu.VMEM((GROUP, SIDE, 2 * SIDE, chans), F32),
            pltpu.VMEM((3, GROUP, SIDE + 2, SIDE, chans), BF16),
            pltpu.VMEM((GROUP * CELLS, chans), BF16),
            pltpu.VMEM((rois, 4, CELLS), F32),
            pltpu.VMEM((WINDOW, SLOTS, 4 * CELLS), F32),
            pltpu.VMEM((WINDOW, SLOTS, 4 * CELLS), F32),
            pltpu.SemaphoreType.DMA((CHUNKS + 5,)),
            pltpu.SemaphoreType.DMA((4,)),
            pltpu.SemaphoreType.DMA((4,)),
            pltpu.SemaphoreType.DMA((rois,)),
            pltpu.SemaphoreType.DMA((rois,)),
            pltpu.SemaphoreType.DMA((WINDOW,)),
            pltpu.SemaphoreType.DMA((WINDOW,)),
            pltpu.SemaphoreType.REGULAR((2,)),
        ],
        compiler_params=pltpu.CompilerParams(
            collective_id=0, has_side_effects=True, vmem_limit_bytes=60 * 1024 * 1024
        ),
    )(
        spots,
        turns,
        counts,
        classes,
        features,
        fpn_weight,
        head_weight,
        deconv_weight,
        class_weight,
    )


def solution(mesh):
    placed = (
        P(("tiles", "rows"), None, None),
        P(("tiles", "rows"), None),
        P(("tiles", "rows"), None),
        P(("tiles", "rows")),
        P(("tiles", "rows")),
        P(),
        P(),
        P(),
        P(),
    )
    return jax.shard_map(
        functools.partial(body, mesh.shape["rows"]),
        mesh=mesh,
        in_specs=placed,
        out_specs=P(("tiles", "rows"), None),
        check_vma=False,
    )
```

```python
import functools

import jax
import jax.numpy as jnp
from jax import lax
from jax.experimental import pallas as pl
from jax.experimental.pallas import tpu as pltpu
from jax.sharding import PartitionSpec as P

SIDE = 16
CELLS = SIDE * SIDE
WINDOW = 4
SLOTS = 2
EDGE = 16
LOW = 3
CHUNKS = 4
MESH = pl.DeviceIdType.MESH
BF16, F32 = jnp.bfloat16, jnp.float32


def turn_of(is_last, offset):
    return jnp.where(
        jnp.logical_and(is_last, offset > 0), offset - 1, WINDOW - 1 - offset
    )


def offset_of(is_last, turn):
    return jnp.where(
        jnp.logical_and(is_last, turn < WINDOW - 1), turn + 1, WINDOW - 1 - turn
    )


def order_of(is_last, offsets, corners, order, cols, rois):
    held = [offsets[0, q] for q in range(rois)]
    place = []
    for q in range(rois):
        rank = jnp.int32(0)
        for p in range(q):
            rank = rank + (held[p] == held[q]).astype(jnp.int32)
        place.append(turn_of(is_last, held[q]) * SLOTS + rank)
    for p in range(rois):
        slot = jnp.int32(0)
        for q in range(1, rois):
            slot = jnp.where(place[q] == p, q, slot)
        order[p] = slot
        cols[0, p] = corners[1, slot]


def kernel(
    count,
    corners_sm,
    offset_sm,
    count_sm,
    class_sm,
    feat,
    fpn_hbm,
    head_hbm,
    dec_hbm,
    cls_w,
    out,
    band,
    wide,
    fpn_w,
    head_w,
    dec_w,
    dec_t,
    order,
    cols,
    near_cols,
    table,
    below_row,
    sent,
    got,
    row_sent,
    row_got,
    low_sent,
    low_got,
    ends,
    joined,
    wins,
    blocks,
    shifted,
    hidden,
    logits,
    outgoing,
    incoming,
    extra_got,
    load_sem,
    small_send,
    small_recv,
    piece_send,
    piece_recv,
    mask_send,
    mask_recv,
    ready,
):
    me = lax.axis_index("rows")
    rois = sent.shape[0]
    band_rows, columns, chans = band.shape
    rest = band_rows - 1
    halves, lanes = wide.shape[0], wide.shape[-1]
    has_up = me > 0
    has_down = me < count - 1
    even = lax.rem(me, 2) == 0
    cut = jnp.logical_and(jnp.logical_not(even), has_down)
    helps = jnp.logical_and(even, has_up)
    helper = lax.rem(me + count - 2, count)
    helped = jnp.logical_and(lax.rem(helper, 2) == 0, helper > 0)
    first_sent = jnp.where(helps, SLOTS, 0)
    first_join = jnp.where(cut, SLOTS, 0)

    def at(step):
        return {"rows": lax.rem(me + step + count, count)}

    barrier = pltpu.get_barrier_semaphore()
    is_last = me == count - 1
    pl.semaphore_signal(barrier, inc=1, device_id=at(-1), device_id_type=MESH)

    @pl.when(has_down)
    def _():
        pl.semaphore_signal(barrier, inc=1, device_id=at(1), device_id_type=MESH)

    def tell(k, step):
        pl.semaphore_signal(ready.at[k], inc=1, device_id=at(step), device_id_type=MESH)

    chunk = band_rows // CHUNKS
    band_loads = [
        pltpu.make_async_copy(
            feat.at[pl.ds(c * chunk, chunk)], band.at[pl.ds(c * chunk, chunk)], load_sem.at[c]
        )
        for c in range(CHUNKS)
    ]
    loads = [
        pltpu.make_async_copy(fpn_hbm, fpn_w, load_sem.at[CHUNKS]),
        pltpu.make_async_copy(head_hbm, head_w, load_sem.at[CHUNKS + 1]),
        pltpu.make_async_copy(dec_hbm, dec_w, load_sem.at[CHUNKS + 2]),
    ]
    for load in band_loads + loads:
        load.start()

    order_of(is_last, offset_sm, corners_sm, order, cols, rois)
    limit = jnp.where(has_down, 2 * band_rows, band_rows)

    def enter(p, top, class_id, first, last, rows):
        for k, entry in enumerate((top, class_id, first, last, rows)):
            table[k, p] = entry

    for p in range(rois):
        slot = order[p]
        top = lax.rem(corners_sm[0, slot], band_rows)
        live = (slot < count_sm[0]).astype(jnp.int32)
        last = live * SIDE
        if p < SLOTS:
            last = jnp.where(cut, live * jnp.minimum(band_rows - 1 - top, SIDE), last)
            for k, entry in enumerate((top, class_sm[slot], live)):
                cols[0, rois + 3 * p + k] = entry
        enter(p, top, class_sm[slot], 0, last, limit)

    pl.semaphore_wait(barrier, jnp.where(has_up, 2, 1))

    first_row = pltpu.make_async_remote_copy(
        src_ref=feat.at[pl.ds(0, 1)],
        dst_ref=below_row,
        send_sem=small_send.at[3],
        recv_sem=small_recv.at[3],
        device_id=at(-1),
        device_id_type=MESH,
    )

    smalls = [
        pltpu.make_async_remote_copy(
            src_ref=cols,
            dst_ref=near_cols.at[side],
            send_sem=small_send.at[side],
            recv_sem=small_recv.at[side],
            device_id=at(1 - 2 * side),
            device_id_type=MESH,
        )
        for side in range(2)
    ]

    @pl.when(has_down)
    def _():
        smalls[0].start()

    @pl.when(has_up)
    def _():
        smalls[1].start()
        first_row.start()

    @pl.when(has_up)
    def _():
        tell(0, -1)

    @pl.when(is_last)
    def _():
        tell(2, 1)

    wide[:, :, 0:EDGE, :] = jnp.zeros((halves, band_rows + 1, EDGE, lanes), F32)
    wide[:, :, EDGE + columns :, :] = jnp.zeros((halves, band_rows + 1, EDGE, lanes), F32)

    for c in range(CHUNKS):
        band_loads[c].wait()

        def widen(i, carry):
            for h in range(halves):
                wide[h, pl.ds(i, 1), EDGE : EDGE + columns, :] = band[
                    pl.ds(i, 1), :, h * lanes : (h + 1) * lanes
                ].astype(F32)
            return carry

        lax.fori_loop(c * chunk, (c + 1) * chunk, widen, 0)

    def piece(p):
        return pltpu.make_async_remote_copy(
            src_ref=sent.at[p],
            dst_ref=got.at[p],
            send_sem=piece_send.at[p],
            recv_sem=piece_recv.at[p],
            device_id=at(-1),
            device_id_type=MESH,
        )

    row_copy = pltpu.make_async_remote_copy(
        src_ref=row_sent,
        dst_ref=row_got,
        send_sem=small_send.at[2],
        recv_sem=small_recv.at[2],
        device_id=at(1),
        device_id_type=MESH,
    )

    low_copy = pltpu.make_async_remote_copy(
        src_ref=low_sent,
        dst_ref=low_got,
        send_sem=small_send.at[4],
        recv_sem=small_recv.at[4],
        device_id=at(1),
        device_id_type=MESH,
    )
    lows = SLOTS * LOW

    @pl.when(cut)
    def _():
        for h in range(halves):
            part = slice(h * lanes, (h + 1) * lanes)
            sides = [[], []]
            for k in range(lows):
                row = band_rows - LOW + k % LOW
                start = cols[0, k // LOW] + (EDGE - 1)
                low_sent[k, :, part] = wide[h, row, pl.ds(start + 1, SIDE), :].astype(BF16)
                sides[0].append(wide[h, row, pl.ds(start, 1), :])
                sides[1].append(wide[h, row, pl.ds(start + SIDE + 1, 1), :])
            spare = [jnp.zeros((SIDE - 2 * lows, lanes), F32)]
            low_sent[lows, :, part] = jnp.concatenate(sides[0] + sides[1] + spare, axis=0).astype(
                BF16
            )
        low_copy.start()

    @pl.when(has_down)
    def _():
        smalls[1].wait_recv()

        for h in range(halves):
            part = slice(h * lanes, (h + 1) * lanes)
            sides = [[], []]
            for p in range(rois):
                start = near_cols[1, 0, p] + (EDGE - 1)
                row_sent[p, :, part] = wide[h, band_rows - 1, pl.ds(start + 1, SIDE), :].astype(
                    BF16
                )
                sides[0].append(wide[h, band_rows - 1, pl.ds(start, 1), :])
                sides[1].append(wide[h, band_rows - 1, pl.ds(start + SIDE + 1, 1), :])
            row_sent[rois, :, part] = jnp.concatenate(sides[0] + sides[1], axis=0).astype(BF16)
        row_copy.start()

    @pl.when(has_up)
    def _():
        smalls[0].wait_recv()

        def gather(p, carry):
            start = near_cols[0, 0, p] + (EDGE - 1)
            for h in range(halves):
                part = slice(h * lanes, (h + 1) * lanes)
                sent[p, 0:rest, :, part] = wide[
                    h, 1:band_rows, pl.ds(start + 1, SIDE), :
                ].astype(BF16)
                for i in range(rest):
                    ends[0, i : i + 1, part] = wide[h, i + 1, pl.ds(start, 1), :]
                    ends[1, i : i + 1, part] = wide[h, i + 1, pl.ds(start + SIDE + 1, 1), :]
            sent[p, rest:] = ends[...].astype(BF16)
            piece(p).start()
            return carry

        lax.fori_loop(first_sent, rois, gather, 0)

    @pl.when(has_down)
    def _():
        pl.semaphore_wait(ready.at[0], 1)

    @pl.when(jnp.logical_and(has_up, has_down))
    def _():
        tell(1, -1)

    @pl.when(has_down)
    def _():
        first_row.wait_recv()

    @pl.when(jnp.logical_not(has_down))
    def _():
        below_row[...] = jnp.zeros_like(below_row)

    for h in range(halves):
        wide[h, band_rows :, EDGE : EDGE + columns, :] = below_row[
            :, :, h * lanes : (h + 1) * lanes
        ].astype(F32)

    def own(p, carry):
        start = cols[0, p] + (EDGE - 1)
        for dj in range(3):
            for h in range(halves):
                wins[p, dj, 1 : band_rows + 2, :, h * lanes : (h + 1) * lanes] = wide[
                    h, :, pl.ds(start + dj, SIDE), :
                ].astype(BF16)
        return carry

    lax.fori_loop(0, rois, own, 0)

    @pl.when(jnp.logical_not(helped))
    def _():
        extra_got[...] = jnp.zeros_like(extra_got)

    wins[0:SLOTS, :, band_rows + 2 :] = jnp.zeros(
        (SLOTS, 3, rest, SIDE, chans), BF16
    )
    blocks[...] = jnp.zeros_like(blocks)
    for u in range(SLOTS):
        for dj in range(3):
            shifted[dj, u, 0] = jnp.zeros((SIDE, chans), BF16)
            shifted[dj, u, SIDE + 1] = jnp.zeros((SIDE, chans), BF16)

    @pl.when(jnp.logical_not(has_down))
    def _():
        got[...] = jnp.zeros_like(got)

    for load in loads:
        load.wait()
    for yx in range(4):
        dec_t[yx * chans : (yx + 1) * chans] = jnp.transpose(
            dec_w[:, yx * chans : (yx + 1) * chans]
        )

    def mask(f):
        return pltpu.make_async_remote_copy(
            src_ref=outgoing.at[f],
            dst_ref=incoming.at[f],
            send_sem=mask_send.at[f],
            recv_sem=mask_recv.at[f],
            device_id=at(f),
            device_id_type=MESH,
        )

    def join(p, carry):
        @pl.when(has_down)
        def _():
            piece(p).wait_recv()

        joined[0:rest, 8 : 8 + SIDE, :] = got[p, 0:rest].astype(F32)
        ends[...] = got[p, rest:].astype(F32)
        for i in range(rest):
            joined[i, 7:8, :] = ends[0, i : i + 1, :]
            joined[i, 8 + SIDE : 9 + SIDE, :] = ends[1, i : i + 1, :]
        wins[p, 0, band_rows + 2 :] = joined[0:rest, 7 : 7 + SIDE, :].astype(BF16)
        wins[p, 1, band_rows + 2 :] = got[p, 0:rest]
        wins[p, 2, band_rows + 2 :] = joined[0:rest, 9 : 9 + SIDE, :].astype(BF16)
        return carry

    def fpn(size, base, carry):
        tops = [table[0, base + u] for u in range(size)]
        lhs = jnp.concatenate(
            [
                jnp.concatenate(
                    [
                        wins[base + u, tap % 3, pl.ds(tops[u] + tap // 3, SIDE)].reshape(
                            CELLS, chans
                        )
                        for u in range(size)
                    ],
                    axis=0,
                )
                for tap in range(9)
            ],
            axis=1,
        )
        total = jnp.dot(lhs, fpn_w[...], preferred_element_type=F32)
        total = total.reshape(size, SIDE, SIDE, chans)
        row = lax.broadcasted_iota(jnp.int32, (SIDE, SIDE, chans), 0)
        for u in range(size):
            kept = jnp.where(row + tops[u] < table[4, base + u], total[u], 0.0)
            blocks[u, :, 8 : 8 + SIDE, :] = kept
            shifted[1, u, 1 : 1 + SIDE] = kept.astype(BF16)
        for u in range(size):
            for dj in (0, 2):
                shifted[dj, u, 1 : 1 + SIDE] = blocks[u, :, 7 + dj : 7 + dj + SIDE, :].astype(BF16)
        return carry

    def head(size, base, carry):
        lhs = jnp.concatenate(
            [
                shifted[tap % 3, 0:size, tap // 3 : tap // 3 + SIDE].reshape(size * CELLS, chans)
                for tap in range(9)
            ],
            axis=1,
        )
        total = jnp.dot(lhs, head_w[...], preferred_element_type=F32)
        hidden[0 : size * CELLS] = jnp.maximum(total, 0.0).astype(BF16)
        return carry

    def tail(size, base, carry):
        for u in range(size):
            rows = cls_w[...].astype(F32)
            which = lax.broadcasted_iota(jnp.int32, rows.shape, 0)
            chosen = jnp.sum(
                jnp.where(which == table[1, base + u], rows, 0.0), axis=0, keepdims=True
            )
            column = jnp.transpose(jnp.broadcast_to(chosen, (lanes, chans)))
            made = []
            for yx in range(4):
                up = lax.dot_general(
                    dec_t[yx * chans : (yx + 1) * chans],
                    hidden[u * CELLS : (u + 1) * CELLS],
                    (((1,), (1,)), ((), ())),
                    preferred_element_type=F32,
                )
                up = jnp.maximum(up, 0.0).astype(BF16).astype(F32)
                for v in range(CELLS // lanes):
                    part = slice(v * lanes, (v + 1) * lanes)
                    logit = jnp.sum(up[:, part] * column, axis=0, keepdims=True)
                    high = (v * lanes + lax.broadcasted_iota(jnp.int32, (1, lanes), 1)) // SIDE
                    kept = (high >= table[2, base + u]) & (high < table[3, base + u])
                    made.append(jnp.where(kept, logit, 0.0))
            count_of = CELLS // lanes
            logits[base + u] = jnp.concatenate(
                [
                    jnp.concatenate(made[yx * count_of : (yx + 1) * count_of], axis=1)
                    for yx in range(4)
                ],
                axis=0,
            )
        return carry

    def spread(g, to):
        shape = (4 * SLOTS, lanes)
        lane = lax.broadcasted_iota(jnp.int32, shape, 1)
        held = lax.broadcasted_iota(jnp.int32, shape, 0) % 4
        mine = (lane // (2 * SIDE)) % 2 * 2 + lane % 2 == held
        span = lanes // (4 * SIDE)
        made = []
        pair = logits[pl.ds(g * SLOTS, SLOTS)].reshape(4 * SLOTS, CELLS)
        for k in range(4 * CELLS // lanes):
            v, first = divmod(k * span * SIDE, lanes)
            index = first + lane // (4 * SIDE) * SIDE + lane % (2 * SIDE) // 2
            picked = jnp.take_along_axis(
                pair[:, v * lanes : (v + 1) * lanes], index, axis=1, mode="promise_in_bounds"
            )
            picked = jnp.where(mine, picked, 0.0).reshape(SLOTS, 4, lanes)
            made.append(jnp.sum(picked, axis=1))
        to[...] = jnp.concatenate(made, axis=1)

    def stages(size, base):
        for stage in (fpn, head, tail):
            lax.fori_loop(base, base + 1, functools.partial(stage, size), 0)

    extra = pltpu.make_async_remote_copy(
        src_ref=outgoing.at[WINDOW],
        dst_ref=extra_got,
        send_sem=mask_send.at[0],
        recv_sem=mask_recv.at[0],
        device_id=at(2),
        device_id_type=MESH,
    )

    @pl.when(helps)
    def _():
        wins[rois:, :, 0 : band_rows + 1 - LOW] = jnp.zeros(
            (SLOTS, 3, band_rows + 1 - LOW, SIDE, chans), BF16
        )
        for u in range(SLOTS):
            top, class_id, live = [near_cols[0, 0, rois + 3 * u + k] for k in range(3)]
            enter(rois + u, top, class_id, band_rows - 1 - top, live * SIDE, 2 * band_rows)
            start = near_cols[0, 0, u] + (EDGE - 1)
            for dj in range(3):
                for h in range(halves):
                    wins[rois + u, dj, band_rows + 1 :, :, h * lanes : (h + 1) * lanes] = wide[
                        h, 0:band_rows, pl.ds(start + dj, SIDE), :
                    ].astype(BF16)
        low_copy.wait_recv()
        joined[0:lows, 8 : 8 + SIDE, :] = low_got[0:lows].astype(F32)
        ends[0] = low_got[lows].astype(F32)
        for k in range(lows):
            joined[k, 7:8, :] = ends[0, k : k + 1, :]
            joined[k, 8 + SIDE : 9 + SIDE, :] = ends[0, lows + k : lows + k + 1, :]
        for u in range(SLOTS):
            for dj in range(3):
                wins[rois + u, dj, band_rows + 1 - LOW : band_rows + 1] = joined[
                    u * LOW : (u + 1) * LOW, 7 + dj : 7 + dj + SIDE, :
                ].astype(BF16)

    def above():
        @pl.when(has_up)
        def _():
            row_copy.wait_recv()

        @pl.when(jnp.logical_not(has_up))
        def _():
            row_got[...] = jnp.zeros_like(row_got)

        joined[0:rois, 8 : 8 + SIDE, :] = row_got[0:rois].astype(F32)
        ends[0] = row_got[rois].astype(F32)
        for p in range(rois):
            joined[p, 7:8, :] = ends[0, p : p + 1, :]
            joined[p, 8 + SIDE : 9 + SIDE, :] = ends[0, rois + p : rois + p + 1, :]
        for dj in range(3):
            wins[0:rois, dj, 0] = joined[0:rois, 7 + dj : 7 + dj + SIDE, :].astype(BF16)

    def pair(turn, carry):
        own_turn = turn >= 0
        base = jnp.where(own_turn, turn * SLOTS, rois)

        @pl.when(turn == 0)
        def _():
            above()

        start = jnp.where(own_turn, jnp.maximum(base, first_join), base + SLOTS)
        lax.fori_loop(start, base + SLOTS, join, 0)
        stages(SLOTS, base)
        f = jnp.where(own_turn, offset_of(is_last, turn), WINDOW)
        spread(jnp.where(own_turn, turn, WINDOW), outgoing.at[f])

        @pl.when(jnp.logical_and(turn == 0, has_down))
        def _():
            pl.semaphore_wait(ready.at[1], 1)

        @pl.when(jnp.logical_and(own_turn, f > 0))
        def _():
            mask(f).start()

        @pl.when(jnp.logical_not(own_turn))
        def _():
            extra.start()

        @pl.when(jnp.logical_and(turn == 0, is_last))
        def _():
            pl.semaphore_wait(ready.at[0], 1)
            tell(1, -1)
            pl.semaphore_wait(ready.at[1], 1)

        @pl.when(jnp.logical_and(turn == 1, jnp.logical_not(has_up)))
        def _():
            pl.semaphore_wait(ready.at[2], 1)
            tell(0, -1)
            tell(1, -1)

        return carry

    lax.fori_loop(jnp.where(helps, -1, 0), jnp.where(even, WINDOW, WINDOW - 1), pair, 0)

    @pl.when(jnp.logical_not(even))
    def _():
        def single(p, carry):
            join(p, carry)
            stages(1, p)
            return carry

        lax.fori_loop(rois - SLOTS, rois, single, 0)
        spread(WINDOW - 1, outgoing.at[0])

    out[0:SLOTS] = outgoing[0]
    for f in range(1, WINDOW):
        mask(f).wait_recv()

    @pl.when(helped)
    def _():
        extra.wait_recv()

    for f in range(1, WINDOW - 1):
        out[f * SLOTS : (f + 1) * SLOTS] = incoming[f]
    out[(WINDOW - 1) * SLOTS :] = incoming[WINDOW - 1] + extra_got[...]

    for f in range(1, WINDOW):
        mask(f).wait_send()

    @pl.when(helps)
    def _():
        extra.wait_send()

    @pl.when(cut)
    def _():
        low_copy.wait_send()

    @pl.when(has_down)
    def _():
        smalls[0].wait_send()
        row_copy.wait_send()

    @pl.when(has_up)
    def _():
        first_row.wait_send()
        smalls[1].wait_send()

        def drain(p, carry):
            piece(p).wait_send()
            return carry

        lax.fori_loop(first_sent, rois, drain, 0)


def body(
    count,
    features,
    corners,
    offsets,
    counts,
    classes,
    fpn_weight,
    head_weight,
    deconv_weight,
    class_weight,
):
    band_rows, columns, chans = features.shape
    rois = corners.shape[0]
    spots = corners.T
    turns = offsets.T
    smem = pl.BlockSpec(memory_space=pltpu.SMEM)
    vmem = pl.BlockSpec(memory_space=pltpu.VMEM)
    anyw = pl.BlockSpec(memory_space=pl.ANY)
    return pl.pallas_call(
        functools.partial(kernel, count),
        out_shape=jax.ShapeDtypeStruct((WINDOW * SLOTS, 4 * CELLS), F32),
        in_specs=[smem, smem, smem, smem, anyw, anyw, anyw, anyw, vmem],
        out_specs=vmem,
        scratch_shapes=[
            pltpu.VMEM(features.shape, BF16),
            pltpu.VMEM((chans // 128, band_rows + 1, columns + 2 * EDGE, 128), F32),
            pltpu.VMEM(fpn_weight.shape, BF16),
            pltpu.VMEM(head_weight.shape, BF16),
            pltpu.VMEM(deconv_weight.shape, BF16),
            pltpu.VMEM(deconv_weight.shape[::-1], BF16),
            pltpu.SMEM((rois,), jnp.int32),
            pltpu.SMEM((1, rois + 3 * SLOTS), jnp.int32),
            pltpu.SMEM((2, 1, rois + 3 * SLOTS), jnp.int32),
            pltpu.SMEM((5, rois + SLOTS), jnp.int32),
            pltpu.VMEM((1, columns, chans), BF16),
            pltpu.VMEM((rois, band_rows + 1, SIDE, chans), BF16),
            pltpu.VMEM((rois, band_rows + 1, SIDE, chans), BF16),
            pltpu.VMEM((rois + 1, SIDE, chans), BF16),
            pltpu.VMEM((rois + 1, SIDE, chans), BF16),
            pltpu.VMEM((SLOTS * LOW + 1, SIDE, chans), BF16),
            pltpu.VMEM((SLOTS * LOW + 1, SIDE, chans), BF16),
            pltpu.VMEM((2, SIDE, chans), F32),
            pltpu.VMEM((SIDE, 2 * SIDE, chans), F32),
            pltpu.VMEM((rois + SLOTS, 3, 2 * band_rows + 1, SIDE, chans), BF16),
            pltpu.VMEM((SLOTS, SIDE, 2 * SIDE, chans), F32),
            pltpu.VMEM((3, SLOTS, SIDE + 2, SIDE, chans), BF16),
            pltpu.VMEM((SLOTS * CELLS, chans), BF16),
            pltpu.VMEM((rois + SLOTS, 4, CELLS), F32),
            pltpu.VMEM((WINDOW + 1, SLOTS, 4 * CELLS), F32),
            pltpu.VMEM((WINDOW, SLOTS, 4 * CELLS), F32),
            pltpu.VMEM((SLOTS, 4 * CELLS), F32),
            pltpu.SemaphoreType.DMA((CHUNKS + 5,)),
            pltpu.SemaphoreType.DMA((5,)),
            pltpu.SemaphoreType.DMA((5,)),
            pltpu.SemaphoreType.DMA((rois,)),
            pltpu.SemaphoreType.DMA((rois,)),
            pltpu.SemaphoreType.DMA((WINDOW,)),
            pltpu.SemaphoreType.DMA((WINDOW,)),
            pltpu.SemaphoreType.REGULAR((3,)),
        ],
        compiler_params=pltpu.CompilerParams(
            collective_id=0, has_side_effects=True, vmem_limit_bytes=60 * 1024 * 1024
        ),
    )(
        spots,
        turns,
        counts,
        classes,
        features,
        fpn_weight,
        head_weight,
        deconv_weight,
        class_weight,
    )


def solution(mesh):
    placed = (
        P(("tiles", "rows"), None, None),
        P(("tiles", "rows"), None),
        P(("tiles", "rows"), None),
        P(("tiles", "rows")),
        P(("tiles", "rows")),
        P(),
        P(),
        P(),
        P(),
    )
    return jax.shard_map(
        functools.partial(body, mesh.shape["rows"]),
        mesh=mesh,
        in_specs=placed,
        out_specs=P(("tiles", "rows"), None),
        check_vma=False,
    )
```

```python
import functools

import jax
import jax.numpy as jnp
from jax import lax
from jax.experimental import pallas as pl
from jax.experimental.pallas import tpu as pltpu
from jax.sharding import PartitionSpec as P

SIDE = 16
CELLS = SIDE * SIDE
WINDOW = 4
SLOTS = 2
EDGE = 16
LOW = 3
CHUNKS = 4
MESH = pl.DeviceIdType.MESH
BF16, F32 = jnp.bfloat16, jnp.float32


def turn_of(kind, offset):
    odd, is_last, is_next = kind
    turn = WINDOW - 1 - offset
    turn = jnp.where(jnp.logical_and(is_next, turn < 2), 1 - turn, turn)
    turn = jnp.where(odd, jnp.where(offset == 1, 0, WINDOW - offset), turn)
    turn = jnp.where(is_last, offset - 1, turn)
    return jnp.where(offset == 0, WINDOW - 1, turn)


def offset_of(kind, turn):
    odd, is_last, is_next = kind
    offset = WINDOW - 1 - jnp.where(jnp.logical_and(is_next, turn < 2), 1 - turn, turn)
    offset = jnp.where(odd, jnp.where(turn == 0, 1, WINDOW - turn), offset)
    offset = jnp.where(is_last, turn + 1, offset)
    return jnp.where(turn == WINDOW - 1, 0, offset)


def order_of(kind, offsets, corners, order, cols, rois):
    held = [offsets[0, q] for q in range(rois)]
    place = []
    for q in range(rois):
        rank = jnp.int32(0)
        for p in range(q):
            rank = rank + (held[p] == held[q]).astype(jnp.int32)
        place.append(turn_of(kind, held[q]) * SLOTS + rank)
    for p in range(rois):
        slot = jnp.int32(0)
        for q in range(1, rois):
            slot = jnp.where(place[q] == p, q, slot)
        order[p] = slot
        cols[0, p] = corners[1, slot]


def kernel(
    count,
    corners_sm,
    offset_sm,
    count_sm,
    class_sm,
    feat,
    fpn_hbm,
    head_hbm,
    dec_hbm,
    cls_w,
    out,
    band,
    wide,
    fpn_w,
    head_w,
    dec_w,
    dec_t,
    order,
    cols,
    near_cols,
    table,
    below_row,
    sent,
    got,
    row_sent,
    row_got,
    low_sent,
    low_got,
    ends,
    joined,
    wins,
    blocks,
    shifted,
    hidden,
    logits,
    outgoing,
    incoming,
    load_sem,
    small_send,
    small_recv,
    piece_send,
    piece_recv,
    mask_send,
    mask_recv,
    ready,
):
    me = lax.axis_index("rows")
    rois = sent.shape[0]
    band_rows, columns, chans = band.shape
    rest = band_rows - 1
    halves, lanes = wide.shape[0], wide.shape[-1]
    has_up = me > 0
    has_down = me < count - 1
    even = lax.rem(me, 2) == 0
    cut = jnp.logical_and(jnp.logical_not(even), has_down)
    helps = jnp.logical_and(even, has_up)
    first_sent = jnp.where(helps, SLOTS, 0)
    first_join = jnp.where(cut, SLOTS, 0)

    def at(step):
        return {"rows": lax.rem(me + step + count, count)}

    barrier = pltpu.get_barrier_semaphore()
    is_last = me == count - 1
    is_next = jnp.logical_and(me == count - 2, even)
    kind = (jnp.logical_not(even), is_last, is_next)
    pl.semaphore_signal(barrier, inc=1, device_id=at(-1), device_id_type=MESH)

    @pl.when(has_down)
    def _():
        pl.semaphore_signal(barrier, inc=1, device_id=at(1), device_id_type=MESH)

    def tell(k, step):
        pl.semaphore_signal(ready.at[k], inc=1, device_id=at(step), device_id_type=MESH)

    chunk = band_rows // CHUNKS
    band_loads = [
        pltpu.make_async_copy(
            feat.at[pl.ds(c * chunk, chunk)], band.at[pl.ds(c * chunk, chunk)], load_sem.at[c]
        )
        for c in range(CHUNKS)
    ]
    loads = [
        pltpu.make_async_copy(fpn_hbm, fpn_w, load_sem.at[CHUNKS]),
        pltpu.make_async_copy(head_hbm, head_w, load_sem.at[CHUNKS + 1]),
        pltpu.make_async_copy(dec_hbm, dec_w, load_sem.at[CHUNKS + 2]),
    ]
    for load in band_loads + loads:
        load.start()

    order_of(kind, offset_sm, corners_sm, order, cols, rois)
    limit = jnp.where(has_down, 2 * band_rows, band_rows)

    def enter(p, top, class_id, first, last, rows):
        for k, entry in enumerate((top, class_id, first, last, rows)):
            table[k, p] = entry

    for p in range(rois):
        slot = order[p]
        top = lax.rem(corners_sm[0, slot], band_rows)
        live = (slot < count_sm[0]).astype(jnp.int32)
        last = live * SIDE
        if p < SLOTS:
            last = jnp.where(cut, live * jnp.minimum(band_rows - 1 - top, SIDE), last)
            for k, entry in enumerate((top, class_sm[slot], live)):
                cols[0, rois + 3 * p + k] = entry
        enter(p, top, class_sm[slot], 0, last, limit)

    pl.semaphore_wait(barrier, jnp.where(has_up, 2, 1))

    first_row = pltpu.make_async_remote_copy(
        src_ref=feat.at[pl.ds(0, 1)],
        dst_ref=below_row,
        send_sem=small_send.at[3],
        recv_sem=small_recv.at[3],
        device_id=at(-1),
        device_id_type=MESH,
    )

    smalls = [
        pltpu.make_async_remote_copy(
            src_ref=cols,
            dst_ref=near_cols.at[side],
            send_sem=small_send.at[side],
            recv_sem=small_recv.at[side],
            device_id=at(1 - 2 * side),
            device_id_type=MESH,
        )
        for side in range(2)
    ]

    @pl.when(has_down)
    def _():
        smalls[0].start()

    @pl.when(has_up)
    def _():
        smalls[1].start()
        first_row.start()

    @pl.when(has_up)
    def _():
        tell(0, -1)

    @pl.when(is_last)
    def _():
        tell(2, 1)

    wide[:, :, 0:EDGE, :] = jnp.zeros((halves, band_rows + 1, EDGE, lanes), F32)
    wide[:, :, EDGE + columns :, :] = jnp.zeros((halves, band_rows + 1, EDGE, lanes), F32)

    for c in range(CHUNKS):
        band_loads[c].wait()

        def widen(i, carry):
            for h in range(halves):
                wide[h, pl.ds(i, 1), EDGE : EDGE + columns, :] = band[
                    pl.ds(i, 1), :, h * lanes : (h + 1) * lanes
                ].astype(F32)
            return carry

        lax.fori_loop(c * chunk, (c + 1) * chunk, widen, 0)

    def piece(p):
        return pltpu.make_async_remote_copy(
            src_ref=sent.at[p],
            dst_ref=got.at[p],
            send_sem=piece_send.at[p],
            recv_sem=piece_recv.at[p],
            device_id=at(-1),
            device_id_type=MESH,
        )

    row_copy = pltpu.make_async_remote_copy(
        src_ref=row_sent,
        dst_ref=row_got,
        send_sem=small_send.at[2],
        recv_sem=small_recv.at[2],
        device_id=at(1),
        device_id_type=MESH,
    )

    low_copy = pltpu.make_async_remote_copy(
        src_ref=low_sent,
        dst_ref=low_got,
        send_sem=small_send.at[4],
        recv_sem=small_recv.at[4],
        device_id=at(1),
        device_id_type=MESH,
    )
    lows = SLOTS * LOW

    @pl.when(cut)
    def _():
        for h in range(halves):
            part = slice(h * lanes, (h + 1) * lanes)
            sides = [[], []]
            for k in range(lows):
                row = band_rows - LOW + k % LOW
                start = cols[0, k // LOW] + (EDGE - 1)
                low_sent[k, :, part] = wide[h, row, pl.ds(start + 1, SIDE), :].astype(BF16)
                sides[0].append(wide[h, row, pl.ds(start, 1), :])
                sides[1].append(wide[h, row, pl.ds(start + SIDE + 1, 1), :])
            spare = [jnp.zeros((SIDE - 2 * lows, lanes), F32)]
            low_sent[lows, :, part] = jnp.concatenate(sides[0] + sides[1] + spare, axis=0).astype(
                BF16
            )
        low_copy.start()

    @pl.when(has_down)
    def _():
        smalls[1].wait_recv()

        for h in range(halves):
            part = slice(h * lanes, (h + 1) * lanes)
            sides = [[], []]
            for p in range(rois):
                start = near_cols[1, 0, p] + (EDGE - 1)
                row_sent[p, :, part] = wide[h, band_rows - 1, pl.ds(start + 1, SIDE), :].astype(
                    BF16
                )
                sides[0].append(wide[h, band_rows - 1, pl.ds(start, 1), :])
                sides[1].append(wide[h, band_rows - 1, pl.ds(start + SIDE + 1, 1), :])
            row_sent[rois, :, part] = jnp.concatenate(sides[0] + sides[1], axis=0).astype(BF16)
        row_copy.start()

    @pl.when(has_up)
    def _():
        smalls[0].wait_recv()

        def gather(p, carry):
            start = near_cols[0, 0, p] + (EDGE - 1)
            for h in range(halves):
                part = slice(h * lanes, (h + 1) * lanes)
                sent[p, 0:rest, :, part] = wide[
                    h, 1:band_rows, pl.ds(start + 1, SIDE), :
                ].astype(BF16)
                for i in range(rest):
                    ends[0, i : i + 1, part] = wide[h, i + 1, pl.ds(start, 1), :]
                    ends[1, i : i + 1, part] = wide[h, i + 1, pl.ds(start + SIDE + 1, 1), :]
            sent[p, rest:] = ends[...].astype(BF16)
            piece(p).start()
            return carry

        lax.fori_loop(first_sent, rois, gather, 0)

    @pl.when(has_down)
    def _():
        pl.semaphore_wait(ready.at[0], 1)

    @pl.when(jnp.logical_and(has_up, has_down))
    def _():
        tell(1, -1)

    @pl.when(has_down)
    def _():
        first_row.wait_recv()

    @pl.when(jnp.logical_not(has_down))
    def _():
        below_row[...] = jnp.zeros_like(below_row)

    for h in range(halves):
        wide[h, band_rows :, EDGE : EDGE + columns, :] = below_row[
            :, :, h * lanes : (h + 1) * lanes
        ].astype(F32)

    def own(p, carry):
        start = cols[0, p] + (EDGE - 1)
        for dj in range(3):
            for h in range(halves):
                wins[p, dj, 1 : band_rows + 2, :, h * lanes : (h + 1) * lanes] = wide[
                    h, :, pl.ds(start + dj, SIDE), :
                ].astype(BF16)
        return carry

    lax.fori_loop(0, rois, own, 0)

    outgoing[WINDOW] = jnp.zeros(outgoing.shape[1:], F32)

    wins[0:SLOTS, :, band_rows + 2 :] = jnp.zeros(
        (SLOTS, 3, rest, SIDE, chans), BF16
    )
    blocks[...] = jnp.zeros_like(blocks)
    for u in range(SLOTS):
        for dj in range(3):
            shifted[dj, u, 0] = jnp.zeros((SIDE, chans), BF16)
            shifted[dj, u, SIDE + 1] = jnp.zeros((SIDE, chans), BF16)

    @pl.when(jnp.logical_not(has_down))
    def _():
        got[...] = jnp.zeros_like(got)

    for load in loads:
        load.wait()
    for yx in range(4):
        dec_t[yx * chans : (yx + 1) * chans] = jnp.transpose(
            dec_w[:, yx * chans : (yx + 1) * chans]
        )

    def mask(f):
        return pltpu.make_async_remote_copy(
            src_ref=outgoing.at[f],
            dst_ref=incoming.at[f],
            send_sem=mask_send.at[f],
            recv_sem=mask_recv.at[f],
            device_id=at(f),
            device_id_type=MESH,
        )

    def join(p, carry):
        @pl.when(has_down)
        def _():
            piece(p).wait_recv()

        joined[0:rest, 8 : 8 + SIDE, :] = got[p, 0:rest].astype(F32)
        ends[...] = got[p, rest:].astype(F32)
        for i in range(rest):
            joined[i, 7:8, :] = ends[0, i : i + 1, :]
            joined[i, 8 + SIDE : 9 + SIDE, :] = ends[1, i : i + 1, :]
        wins[p, 0, band_rows + 2 :] = joined[0:rest, 7 : 7 + SIDE, :].astype(BF16)
        wins[p, 1, band_rows + 2 :] = got[p, 0:rest]
        wins[p, 2, band_rows + 2 :] = joined[0:rest, 9 : 9 + SIDE, :].astype(BF16)
        return carry

    def fpn(size, base, carry):
        tops = [table[0, base + u] for u in range(size)]
        lhs = jnp.concatenate(
            [
                jnp.concatenate(
                    [
                        wins[base + u, tap % 3, pl.ds(tops[u] + tap // 3, SIDE)].reshape(
                            CELLS, chans
                        )
                        for u in range(size)
                    ],
                    axis=0,
                )
                for tap in range(9)
            ],
            axis=1,
        )
        total = jnp.dot(lhs, fpn_w[...], preferred_element_type=F32)
        total = total.reshape(size, SIDE, SIDE, chans)
        row = lax.broadcasted_iota(jnp.int32, (SIDE, SIDE, chans), 0)
        for u in range(size):
            kept = jnp.where(row + tops[u] < table[4, base + u], total[u], 0.0)
            blocks[u, :, 8 : 8 + SIDE, :] = kept
            shifted[1, u, 1 : 1 + SIDE] = kept.astype(BF16)
        for u in range(size):
            for dj in (0, 2):
                shifted[dj, u, 1 : 1 + SIDE] = blocks[u, :, 7 + dj : 7 + dj + SIDE, :].astype(BF16)
        return carry

    def head(size, base, carry):
        lhs = jnp.concatenate(
            [
                shifted[tap % 3, 0:size, tap // 3 : tap // 3 + SIDE].reshape(size * CELLS, chans)
                for tap in range(9)
            ],
            axis=1,
        )
        total = jnp.dot(lhs, head_w[...], preferred_element_type=F32)
        hidden[0 : size * CELLS] = jnp.maximum(total, 0.0).astype(BF16)
        return carry

    def tail(size, base, carry):
        for u in range(size):
            rows = cls_w[...].astype(F32)
            which = lax.broadcasted_iota(jnp.int32, rows.shape, 0)
            chosen = jnp.sum(
                jnp.where(which == table[1, base + u], rows, 0.0), axis=0, keepdims=True
            )
            column = jnp.transpose(jnp.broadcast_to(chosen, (lanes, chans)))
            made = []
            for yx in range(4):
                up = lax.dot_general(
                    dec_t[yx * chans : (yx + 1) * chans],
                    hidden[u * CELLS : (u + 1) * CELLS],
                    (((1,), (1,)), ((), ())),
                    preferred_element_type=F32,
                )
                up = jnp.maximum(up, 0.0).astype(BF16).astype(F32)
                for v in range(CELLS // lanes):
                    part = slice(v * lanes, (v + 1) * lanes)
                    logit = jnp.sum(up[:, part] * column, axis=0, keepdims=True)
                    high = (v * lanes + lax.broadcasted_iota(jnp.int32, (1, lanes), 1)) // SIDE
                    kept = (high >= table[2, base + u]) & (high < table[3, base + u])
                    made.append(jnp.where(kept, logit, 0.0))
            count_of = CELLS // lanes
            logits[base + u] = jnp.concatenate(
                [
                    jnp.concatenate(made[yx * count_of : (yx + 1) * count_of], axis=1)
                    for yx in range(4)
                ],
                axis=0,
            )
        return carry

    def spread(g, to):
        shape = (4 * SLOTS, lanes)
        lane = lax.broadcasted_iota(jnp.int32, shape, 1)
        held = lax.broadcasted_iota(jnp.int32, shape, 0) % 4
        mine = (lane // (2 * SIDE)) % 2 * 2 + lane % 2 == held
        span = lanes // (4 * SIDE)
        made = []
        pair = logits[pl.ds(g * SLOTS, SLOTS)].reshape(4 * SLOTS, CELLS)
        for k in range(4 * CELLS // lanes):
            v, first = divmod(k * span * SIDE, lanes)
            index = first + lane // (4 * SIDE) * SIDE + lane % (2 * SIDE) // 2
            picked = jnp.take_along_axis(
                pair[:, v * lanes : (v + 1) * lanes], index, axis=1, mode="promise_in_bounds"
            )
            picked = jnp.where(mine, picked, 0.0).reshape(SLOTS, 4, lanes)
            made.append(jnp.sum(picked, axis=1))
        to[...] = jnp.concatenate(made, axis=1)

    def stages(size, base):
        for stage in (fpn, head, tail):
            lax.fori_loop(base, base + 1, functools.partial(stage, size), 0)

    @pl.when(helps)
    def _():
        wins[rois:, :, 0 : band_rows + 1 - LOW] = jnp.zeros(
            (SLOTS, 3, band_rows + 1 - LOW, SIDE, chans), BF16
        )
        for u in range(SLOTS):
            top, class_id, live = [near_cols[0, 0, rois + 3 * u + k] for k in range(3)]
            enter(rois + u, top, class_id, band_rows - 1 - top, live * SIDE, 2 * band_rows)
            start = near_cols[0, 0, u] + (EDGE - 1)
            for dj in range(3):
                for h in range(halves):
                    wins[rois + u, dj, band_rows + 1 :, :, h * lanes : (h + 1) * lanes] = wide[
                        h, 0:band_rows, pl.ds(start + dj, SIDE), :
                    ].astype(BF16)
        low_copy.wait_recv()
        joined[0:lows, 8 : 8 + SIDE, :] = low_got[0:lows].astype(F32)
        ends[0] = low_got[lows].astype(F32)
        for k in range(lows):
            joined[k, 7:8, :] = ends[0, k : k + 1, :]
            joined[k, 8 + SIDE : 9 + SIDE, :] = ends[0, lows + k : lows + k + 1, :]
        for u in range(SLOTS):
            for dj in range(3):
                wins[rois + u, dj, band_rows + 1 - LOW : band_rows + 1] = joined[
                    u * LOW : (u + 1) * LOW, 7 + dj : 7 + dj + SIDE, :
                ].astype(BF16)

    def above():
        @pl.when(has_up)
        def _():
            row_copy.wait_recv()

        @pl.when(jnp.logical_not(has_up))
        def _():
            row_got[...] = jnp.zeros_like(row_got)

        joined[0:rois, 8 : 8 + SIDE, :] = row_got[0:rois].astype(F32)
        ends[0] = row_got[rois].astype(F32)
        for p in range(rois):
            joined[p, 7:8, :] = ends[0, p : p + 1, :]
            joined[p, 8 + SIDE : 9 + SIDE, :] = ends[0, rois + p : rois + p + 1, :]
        for dj in range(3):
            wins[0:rois, dj, 0] = joined[0:rois, 7 + dj : 7 + dj + SIDE, :].astype(BF16)

    def pair(step, carry):
        turn = jnp.where(
            jnp.logical_and(is_next, step < 2), jnp.where(step == 1, -1, step + 1), step
        )
        own_turn = turn >= 0
        base = jnp.where(own_turn, turn * SLOTS, rois)

        @pl.when(turn == 0)
        def _():
            above()

        @pl.when(jnp.logical_and(turn == 0, is_last))
        def _():
            pl.semaphore_wait(ready.at[0], 1)
            tell(1, -1)
            pl.semaphore_wait(ready.at[1], 1)

        start = jnp.where(own_turn, jnp.maximum(base, first_join), base + SLOTS)
        lax.fori_loop(start, base + SLOTS, join, 0)
        stages(SLOTS, base)
        f = jnp.where(own_turn, offset_of(kind, turn), WINDOW)
        spread(jnp.where(own_turn, turn, WINDOW), outgoing.at[f])

        @pl.when(jnp.logical_and(turn == jnp.where(is_next, 1, 0), has_down))
        def _():
            pl.semaphore_wait(ready.at[1], 1)

        @pl.when(jnp.logical_and(own_turn, f > 0))
        def _():
            mask(f).start()

        @pl.when(jnp.logical_and(turn == 0, jnp.logical_not(has_up)))
        def _():
            pl.semaphore_wait(ready.at[2], 1)
            tell(0, -1)
            tell(1, -1)

        return carry

    lax.fori_loop(jnp.where(helps, -1, 0), jnp.where(even, WINDOW, WINDOW - 1), pair, 0)

    @pl.when(jnp.logical_not(even))
    def _():
        def single(p, carry):
            join(p, carry)
            stages(1, p)
            return carry

        lax.fori_loop(rois - SLOTS, rois, single, 0)
        spread(WINDOW - 1, outgoing.at[0])

    out[0:SLOTS] = outgoing[0]
    for f in range(1, WINDOW):
        mask(f).wait_recv()

    out[SLOTS : 2 * SLOTS] = incoming[1] + outgoing[WINDOW]
    for f in range(2, WINDOW):
        out[f * SLOTS : (f + 1) * SLOTS] = incoming[f]

    for f in range(1, WINDOW):
        mask(f).wait_send()

    @pl.when(cut)
    def _():
        low_copy.wait_send()

    @pl.when(has_down)
    def _():
        smalls[0].wait_send()
        row_copy.wait_send()

    @pl.when(has_up)
    def _():
        first_row.wait_send()
        smalls[1].wait_send()

        def drain(p, carry):
            piece(p).wait_send()
            return carry

        lax.fori_loop(first_sent, rois, drain, 0)


def body(
    count,
    features,
    corners,
    offsets,
    counts,
    classes,
    fpn_weight,
    head_weight,
    deconv_weight,
    class_weight,
):
    band_rows, columns, chans = features.shape
    rois = corners.shape[0]
    spots = corners.T
    turns = offsets.T
    smem = pl.BlockSpec(memory_space=pltpu.SMEM)
    vmem = pl.BlockSpec(memory_space=pltpu.VMEM)
    anyw = pl.BlockSpec(memory_space=pl.ANY)
    return pl.pallas_call(
        functools.partial(kernel, count),
        out_shape=jax.ShapeDtypeStruct((WINDOW * SLOTS, 4 * CELLS), F32),
        in_specs=[smem, smem, smem, smem, anyw, anyw, anyw, anyw, vmem],
        out_specs=vmem,
        scratch_shapes=[
            pltpu.VMEM(features.shape, BF16),
            pltpu.VMEM((chans // 128, band_rows + 1, columns + 2 * EDGE, 128), F32),
            pltpu.VMEM(fpn_weight.shape, BF16),
            pltpu.VMEM(head_weight.shape, BF16),
            pltpu.VMEM(deconv_weight.shape, BF16),
            pltpu.VMEM(deconv_weight.shape[::-1], BF16),
            pltpu.SMEM((rois,), jnp.int32),
            pltpu.SMEM((1, rois + 3 * SLOTS), jnp.int32),
            pltpu.SMEM((2, 1, rois + 3 * SLOTS), jnp.int32),
            pltpu.SMEM((5, rois + SLOTS), jnp.int32),
            pltpu.VMEM((1, columns, chans), BF16),
            pltpu.VMEM((rois, band_rows + 1, SIDE, chans), BF16),
            pltpu.VMEM((rois, band_rows + 1, SIDE, chans), BF16),
            pltpu.VMEM((rois + 1, SIDE, chans), BF16),
            pltpu.VMEM((rois + 1, SIDE, chans), BF16),
            pltpu.VMEM((SLOTS * LOW + 1, SIDE, chans), BF16),
            pltpu.VMEM((SLOTS * LOW + 1, SIDE, chans), BF16),
            pltpu.VMEM((2, SIDE, chans), F32),
            pltpu.VMEM((SIDE, 2 * SIDE, chans), F32),
            pltpu.VMEM((rois + SLOTS, 3, 2 * band_rows + 1, SIDE, chans), BF16),
            pltpu.VMEM((SLOTS, SIDE, 2 * SIDE, chans), F32),
            pltpu.VMEM((3, SLOTS, SIDE + 2, SIDE, chans), BF16),
            pltpu.VMEM((SLOTS * CELLS, chans), BF16),
            pltpu.VMEM((rois + SLOTS, 4, CELLS), F32),
            pltpu.VMEM((WINDOW + 1, SLOTS, 4 * CELLS), F32),
            pltpu.VMEM((WINDOW, SLOTS, 4 * CELLS), F32),
            pltpu.SemaphoreType.DMA((CHUNKS + 5,)),
            pltpu.SemaphoreType.DMA((5,)),
            pltpu.SemaphoreType.DMA((5,)),
            pltpu.SemaphoreType.DMA((rois,)),
            pltpu.SemaphoreType.DMA((rois,)),
            pltpu.SemaphoreType.DMA((WINDOW,)),
            pltpu.SemaphoreType.DMA((WINDOW,)),
            pltpu.SemaphoreType.REGULAR((3,)),
        ],
        compiler_params=pltpu.CompilerParams(
            collective_id=0, has_side_effects=True, vmem_limit_bytes=60 * 1024 * 1024
        ),
    )(
        spots,
        turns,
        counts,
        classes,
        features,
        fpn_weight,
        head_weight,
        deconv_weight,
        class_weight,
    )


def solution(mesh):
    placed = (
        P(("tiles", "rows"), None, None),
        P(("tiles", "rows"), None),
        P(("tiles", "rows"), None),
        P(("tiles", "rows")),
        P(("tiles", "rows")),
        P(),
        P(),
        P(),
        P(),
    )
    return jax.shard_map(
        functools.partial(body, mesh.shape["rows"]),
        mesh=mesh,
        in_specs=placed,
        out_specs=P(("tiles", "rows"), None),
        check_vma=False,
    )
```

```python
import functools

import jax
import jax.numpy as jnp
from jax import lax
from jax.experimental import pallas as pl
from jax.experimental.pallas import tpu as pltpu
from jax.sharding import PartitionSpec as P

SIDE = 16
CELLS = SIDE * SIDE
WINDOW = 4
SLOTS = 2
EDGE = 16
LOW = 4
CHUNKS = 4
MESH = pl.DeviceIdType.MESH
BF16, F32 = jnp.bfloat16, jnp.float32


def turn_of(kind, offset):
    odd, is_last, is_next = kind
    turn = WINDOW - 1 - offset
    turn = jnp.where(jnp.logical_and(is_next, turn < 2), 1 - turn, turn)
    turn = jnp.where(odd, jnp.where(offset == 1, 0, WINDOW - offset), turn)
    turn = jnp.where(is_last, offset - 1, turn)
    return jnp.where(offset == 0, WINDOW - 1, turn)


def offset_of(kind, turn):
    odd, is_last, is_next = kind
    offset = WINDOW - 1 - jnp.where(jnp.logical_and(is_next, turn < 2), 1 - turn, turn)
    offset = jnp.where(odd, jnp.where(turn == 0, 1, WINDOW - turn), offset)
    offset = jnp.where(is_last, turn + 1, offset)
    return jnp.where(turn == WINDOW - 1, 0, offset)


def order_of(kind, offsets, corners, order, cols, rois):
    held = [offsets[0, q] for q in range(rois)]
    place = []
    for q in range(rois):
        rank = jnp.int32(0)
        for p in range(q):
            rank = rank + (held[p] == held[q]).astype(jnp.int32)
        place.append(turn_of(kind, held[q]) * SLOTS + rank)
    for p in range(rois):
        slot = jnp.int32(0)
        for q in range(1, rois):
            slot = jnp.where(place[q] == p, q, slot)
        order[p] = slot
        cols[0, p] = corners[1, slot]


def kernel(
    count,
    corners_sm,
    offset_sm,
    count_sm,
    class_sm,
    feat,
    fpn_hbm,
    head_hbm,
    dec_hbm,
    cls_w,
    out,
    band,
    wide,
    fpn_w,
    head_w,
    dec_w,
    dec_t,
    order,
    cols,
    near_cols,
    table,
    sent,
    got,
    row_sent,
    row_got,
    low_sent,
    low_got,
    ends,
    joined,
    wins,
    blocks,
    shifted,
    hidden,
    logits,
    outgoing,
    incoming,
    load_sem,
    small_send,
    small_recv,
    piece_send,
    piece_recv,
    mask_send,
    mask_recv,
    ready,
):
    me = lax.axis_index("rows")
    rois = sent.shape[0]
    band_rows, columns, chans = band.shape
    halves, lanes = wide.shape[0], wide.shape[-1]
    has_up = me > 0
    has_down = me < count - 1
    even = lax.rem(me, 2) == 0
    cut = jnp.logical_and(jnp.logical_not(even), has_down)
    helps = jnp.logical_and(even, has_up)
    first_sent = jnp.where(helps, SLOTS, 0)
    first_join = jnp.where(cut, SLOTS, jnp.where(has_down, 0, rois))

    def at(step):
        return {"rows": lax.rem(me + step + count, count)}

    barrier = pltpu.get_barrier_semaphore()
    is_last = me == count - 1
    is_next = jnp.logical_and(me == count - 2, even)
    kind = (jnp.logical_not(even), is_last, is_next)
    pl.semaphore_signal(barrier, inc=1, device_id=at(-1), device_id_type=MESH)

    @pl.when(has_down)
    def _():
        pl.semaphore_signal(barrier, inc=1, device_id=at(1), device_id_type=MESH)

    def tell(k, step):
        pl.semaphore_signal(ready.at[k], inc=1, device_id=at(step), device_id_type=MESH)

    chunk = band_rows // CHUNKS
    band_loads = [
        pltpu.make_async_copy(
            feat.at[pl.ds(c * chunk, chunk)], band.at[pl.ds(c * chunk, chunk)], load_sem.at[c]
        )
        for c in range(CHUNKS)
    ]
    loads = [
        pltpu.make_async_copy(fpn_hbm, fpn_w, load_sem.at[CHUNKS]),
        pltpu.make_async_copy(head_hbm, head_w, load_sem.at[CHUNKS + 1]),
        pltpu.make_async_copy(dec_hbm, dec_w, load_sem.at[CHUNKS + 2]),
    ]
    for load in band_loads + loads:
        load.start()

    order_of(kind, offset_sm, corners_sm, order, cols, rois)
    limit = jnp.where(has_down, 2 * band_rows, band_rows)

    def enter(p, top, class_id, first, last, rows):
        for k, entry in enumerate((top, class_id, first, last, rows)):
            table[k, p] = entry

    for p in range(rois):
        slot = order[p]
        top = lax.rem(corners_sm[0, slot], band_rows)
        live = (slot < count_sm[0]).astype(jnp.int32)
        last = live * SIDE
        if p < SLOTS:
            last = jnp.where(cut, live * jnp.minimum(band_rows - 2 - top, SIDE), last)
            for k, entry in enumerate((top, class_sm[slot], live)):
                cols[0, rois + 3 * p + k] = entry
        enter(p, top, class_sm[slot], 0, last, limit)

    pl.semaphore_wait(barrier, jnp.where(has_up, 2, 1))

    smalls = [
        pltpu.make_async_remote_copy(
            src_ref=cols,
            dst_ref=near_cols.at[side],
            send_sem=small_send.at[side],
            recv_sem=small_recv.at[side],
            device_id=at(1 - 2 * side),
            device_id_type=MESH,
        )
        for side in range(2)
    ]

    @pl.when(has_down)
    def _():
        smalls[0].start()

    @pl.when(has_up)
    def _():
        smalls[1].start()

    @pl.when(has_up)
    def _():
        tell(0, -1)

    @pl.when(is_last)
    def _():
        tell(2, 1)

    wide[:, :, 0:EDGE, :] = jnp.zeros((halves, band_rows, EDGE, lanes), F32)
    wide[:, :, EDGE + columns :, :] = jnp.zeros((halves, band_rows, EDGE, lanes), F32)

    for c in range(CHUNKS):
        band_loads[c].wait()

        def widen(i, carry):
            for h in range(halves):
                wide[h, pl.ds(i, 1), EDGE : EDGE + columns, :] = band[
                    pl.ds(i, 1), :, h * lanes : (h + 1) * lanes
                ].astype(F32)
            return carry

        lax.fori_loop(c * chunk, (c + 1) * chunk, widen, 0)

    def piece(p):
        return pltpu.make_async_remote_copy(
            src_ref=sent.at[p],
            dst_ref=got.at[p],
            send_sem=piece_send.at[p],
            recv_sem=piece_recv.at[p],
            device_id=at(-1),
            device_id_type=MESH,
        )

    row_copy = pltpu.make_async_remote_copy(
        src_ref=row_sent,
        dst_ref=row_got,
        send_sem=small_send.at[2],
        recv_sem=small_recv.at[2],
        device_id=at(1),
        device_id_type=MESH,
    )

    low_copy = pltpu.make_async_remote_copy(
        src_ref=low_sent,
        dst_ref=low_got,
        send_sem=small_send.at[4],
        recv_sem=small_recv.at[4],
        device_id=at(1),
        device_id_type=MESH,
    )
    lows = SLOTS * LOW

    @pl.when(cut)
    def _():
        for h in range(halves):
            part = slice(h * lanes, (h + 1) * lanes)
            sides = [[], []]
            for k in range(lows):
                row = band_rows - LOW + k % LOW
                start = cols[0, k // LOW] + (EDGE - 1)
                low_sent[k, :, part] = wide[h, row, pl.ds(start + 1, SIDE), :].astype(BF16)
                sides[0].append(wide[h, row, pl.ds(start, 1), :])
                sides[1].append(wide[h, row, pl.ds(start + SIDE + 1, 1), :])
            low_sent[lows, :, part] = jnp.concatenate(sides[0] + sides[1], axis=0).astype(BF16)

        low_copy.start()

    @pl.when(has_down)
    def _():
        smalls[1].wait_recv()

        for h in range(halves):
            part = slice(h * lanes, (h + 1) * lanes)
            sides = [[], []]
            for p in range(rois):
                start = near_cols[1, 0, p] + (EDGE - 1)
                row_sent[p, :, part] = wide[h, band_rows - 1, pl.ds(start + 1, SIDE), :].astype(
                    BF16
                )
                sides[0].append(wide[h, band_rows - 1, pl.ds(start, 1), :])
                sides[1].append(wide[h, band_rows - 1, pl.ds(start + SIDE + 1, 1), :])
            row_sent[rois, :, part] = jnp.concatenate(sides[0] + sides[1], axis=0).astype(BF16)
        row_copy.start()

    @pl.when(has_up)
    def _():
        smalls[0].wait_recv()

        def gather(p, carry):
            start = near_cols[0, 0, p] + (EDGE - 1)
            for h in range(halves):
                part = slice(h * lanes, (h + 1) * lanes)
                sent[p, 0:band_rows, :, part] = wide[h, :, pl.ds(start + 1, SIDE), :].astype(BF16)
                for i in range(band_rows):
                    ends[0, i : i + 1, part] = wide[h, i, pl.ds(start, 1), :]
                    ends[1, i : i + 1, part] = wide[h, i, pl.ds(start + SIDE + 1, 1), :]
            sent[p, band_rows:] = ends[...].astype(BF16)
            piece(p).start()
            return carry

        lax.fori_loop(first_sent, rois, gather, 0)

    @pl.when(has_down)
    def _():
        pl.semaphore_wait(ready.at[0], 1)

    @pl.when(jnp.logical_and(has_up, has_down))
    def _():
        tell(1, -1)

    def own(p, carry):
        start = cols[0, p] + (EDGE - 1)
        for dj in range(3):
            for h in range(halves):
                wins[p, dj, 1 : band_rows + 1, :, h * lanes : (h + 1) * lanes] = wide[
                    h, :, pl.ds(start + dj, SIDE), :
                ].astype(BF16)
        return carry

    lax.fori_loop(0, rois, own, 0)

    outgoing[WINDOW] = jnp.zeros(outgoing.shape[1:], F32)

    wins[0:SLOTS, :, band_rows + 1 :] = jnp.zeros(
        (SLOTS, 3, band_rows, SIDE, chans), BF16
    )
    blocks[...] = jnp.zeros_like(blocks)
    for u in range(SLOTS):
        for dj in range(3):
            shifted[dj, u, 0] = jnp.zeros((SIDE, chans), BF16)
            shifted[dj, u, SIDE + 1] = jnp.zeros((SIDE, chans), BF16)

    @pl.when(jnp.logical_not(has_down))
    def _():
        wins[0:rois, :, band_rows + 1 :] = jnp.zeros((rois, 3, band_rows, SIDE, chans), BF16)

    for load in loads:
        load.wait()
    for yx in range(4):
        dec_t[yx * chans : (yx + 1) * chans] = jnp.transpose(
            dec_w[:, yx * chans : (yx + 1) * chans]
        )

    def mask(f):
        return pltpu.make_async_remote_copy(
            src_ref=outgoing.at[f],
            dst_ref=incoming.at[f],
            send_sem=mask_send.at[f],
            recv_sem=mask_recv.at[f],
            device_id=at(f),
            device_id_type=MESH,
        )

    def join(p, carry):
        @pl.when(has_down)
        def _():
            piece(p).wait_recv()

        joined[0:band_rows, 8 : 8 + SIDE, :] = got[p, 0:band_rows].astype(F32)
        ends[...] = got[p, band_rows:].astype(F32)
        for i in range(band_rows):
            joined[i, 7:8, :] = ends[0, i : i + 1, :]
            joined[i, 8 + SIDE : 9 + SIDE, :] = ends[1, i : i + 1, :]
        wins[p, 0, band_rows + 1 :] = joined[0:band_rows, 7 : 7 + SIDE, :].astype(BF16)
        wins[p, 1, band_rows + 1 :] = got[p, 0:band_rows]
        wins[p, 2, band_rows + 1 :] = joined[0:band_rows, 9 : 9 + SIDE, :].astype(BF16)
        return carry

    def fpn(size, base, carry):
        tops = [table[0, base + u] for u in range(size)]
        lhs = jnp.concatenate(
            [
                jnp.concatenate(
                    [
                        wins[base + u, tap % 3, pl.ds(tops[u] + tap // 3, SIDE)].reshape(
                            CELLS, chans
                        )
                        for u in range(size)
                    ],
                    axis=0,
                )
                for tap in range(9)
            ],
            axis=1,
        )
        total = jnp.dot(lhs, fpn_w[...], preferred_element_type=F32)
        total = total.reshape(size, SIDE, SIDE, chans)
        row = lax.broadcasted_iota(jnp.int32, (SIDE, SIDE, chans), 0)
        for u in range(size):
            kept = jnp.where(row + tops[u] < table[4, base + u], total[u], 0.0)
            blocks[u, :, 8 : 8 + SIDE, :] = kept
            shifted[1, u, 1 : 1 + SIDE] = kept.astype(BF16)
        for u in range(size):
            for dj in (0, 2):
                shifted[dj, u, 1 : 1 + SIDE] = blocks[u, :, 7 + dj : 7 + dj + SIDE, :].astype(BF16)
        return carry

    def head(size, base, carry):
        lhs = jnp.concatenate(
            [
                shifted[tap % 3, 0:size, tap // 3 : tap // 3 + SIDE].reshape(size * CELLS, chans)
                for tap in range(9)
            ],
            axis=1,
        )
        total = jnp.dot(lhs, head_w[...], preferred_element_type=F32)
        hidden[0 : size * CELLS] = jnp.maximum(total, 0.0).astype(BF16)
        return carry

    def tail(size, base, carry):
        for u in range(size):
            rows = cls_w[...].astype(F32)
            which = lax.broadcasted_iota(jnp.int32, rows.shape, 0)
            chosen = jnp.sum(
                jnp.where(which == table[1, base + u], rows, 0.0), axis=0, keepdims=True
            )
            column = jnp.transpose(jnp.broadcast_to(chosen, (lanes, chans)))
            made = []
            for yx in range(4):
                up = lax.dot_general(
                    dec_t[yx * chans : (yx + 1) * chans],
                    hidden[u * CELLS : (u + 1) * CELLS],
                    (((1,), (1,)), ((), ())),
                    preferred_element_type=F32,
                )
                up = jnp.maximum(up, 0.0).astype(BF16).astype(F32)
                for v in range(CELLS // lanes):
                    part = slice(v * lanes, (v + 1) * lanes)
                    logit = jnp.sum(up[:, part] * column, axis=0, keepdims=True)
                    high = (v * lanes + lax.broadcasted_iota(jnp.int32, (1, lanes), 1)) // SIDE
                    kept = (high >= table[2, base + u]) & (high < table[3, base + u])
                    made.append(jnp.where(kept, logit, 0.0))
            count_of = CELLS // lanes
            logits[base + u] = jnp.concatenate(
                [
                    jnp.concatenate(made[yx * count_of : (yx + 1) * count_of], axis=1)
                    for yx in range(4)
                ],
                axis=0,
            )
        return carry

    def spread(g, to):
        shape = (4 * SLOTS, lanes)
        lane = lax.broadcasted_iota(jnp.int32, shape, 1)
        held = lax.broadcasted_iota(jnp.int32, shape, 0) % 4
        mine = (lane // (2 * SIDE)) % 2 * 2 + lane % 2 == held
        span = lanes // (4 * SIDE)
        made = []
        pair = logits[pl.ds(g * SLOTS, SLOTS)].reshape(4 * SLOTS, CELLS)
        for k in range(4 * CELLS // lanes):
            v, first = divmod(k * span * SIDE, lanes)
            index = first + lane // (4 * SIDE) * SIDE + lane % (2 * SIDE) // 2
            picked = jnp.take_along_axis(
                pair[:, v * lanes : (v + 1) * lanes], index, axis=1, mode="promise_in_bounds"
            )
            picked = jnp.where(mine, picked, 0.0).reshape(SLOTS, 4, lanes)
            made.append(jnp.sum(picked, axis=1))
        to[...] = jnp.concatenate(made, axis=1)

    def stages(size, base):
        for stage in (fpn, head, tail):
            lax.fori_loop(base, base + 1, functools.partial(stage, size), 0)

    @pl.when(helps)
    def _():
        wins[rois:, :, 0 : band_rows + 1 - LOW] = jnp.zeros(
            (SLOTS, 3, band_rows + 1 - LOW, SIDE, chans), BF16
        )
        for u in range(SLOTS):
            top, class_id, live = [near_cols[0, 0, rois + 3 * u + k] for k in range(3)]
            enter(rois + u, top, class_id, band_rows - 2 - top, live * SIDE, 2 * band_rows)
            start = near_cols[0, 0, u] + (EDGE - 1)
            for dj in range(3):
                for h in range(halves):
                    wins[rois + u, dj, band_rows + 1 :, :, h * lanes : (h + 1) * lanes] = wide[
                        h, 0:band_rows, pl.ds(start + dj, SIDE), :
                    ].astype(BF16)
        low_copy.wait_recv()
        joined[0:lows, 8 : 8 + SIDE, :] = low_got[0:lows].astype(F32)
        ends[0] = low_got[lows].astype(F32)
        for k in range(lows):
            joined[k, 7:8, :] = ends[0, k : k + 1, :]
            joined[k, 8 + SIDE : 9 + SIDE, :] = ends[0, lows + k : lows + k + 1, :]
        for u in range(SLOTS):
            for dj in range(3):
                wins[rois + u, dj, band_rows + 1 - LOW : band_rows + 1] = joined[
                    u * LOW : (u + 1) * LOW, 7 + dj : 7 + dj + SIDE, :
                ].astype(BF16)

    def above():
        @pl.when(has_up)
        def _():
            row_copy.wait_recv()

        @pl.when(jnp.logical_not(has_up))
        def _():
            row_got[...] = jnp.zeros_like(row_got)

        joined[0:rois, 8 : 8 + SIDE, :] = row_got[0:rois].astype(F32)
        ends[0] = row_got[rois].astype(F32)
        for p in range(rois):
            joined[p, 7:8, :] = ends[0, p : p + 1, :]
            joined[p, 8 + SIDE : 9 + SIDE, :] = ends[0, rois + p : rois + p + 1, :]
        for dj in range(3):
            wins[0:rois, dj, 0] = joined[0:rois, 7 + dj : 7 + dj + SIDE, :].astype(BF16)

    def pair(step, carry):
        turn = jnp.where(
            jnp.logical_and(is_next, step < 2), jnp.where(step == 1, -1, step + 1), step
        )
        own_turn = turn >= 0
        base = jnp.where(own_turn, turn * SLOTS, rois)

        @pl.when(turn == 0)
        def _():
            above()

        @pl.when(jnp.logical_and(turn == 0, is_last))
        def _():
            pl.semaphore_wait(ready.at[0], 1)
            tell(1, -1)
            pl.semaphore_wait(ready.at[1], 1)

        start = jnp.where(own_turn, jnp.maximum(base, first_join), base + SLOTS)
        lax.fori_loop(start, base + SLOTS, join, 0)
        stages(SLOTS, base)
        f = jnp.where(own_turn, offset_of(kind, turn), WINDOW)
        spread(jnp.where(own_turn, turn, WINDOW), outgoing.at[f])

        @pl.when(jnp.logical_and(turn == jnp.where(is_next, 1, 0), has_down))
        def _():
            pl.semaphore_wait(ready.at[1], 1)

        @pl.when(jnp.logical_and(own_turn, f > 0))
        def _():
            mask(f).start()

        @pl.when(jnp.logical_and(turn == 0, jnp.logical_not(has_up)))
        def _():
            pl.semaphore_wait(ready.at[2], 1)
            tell(0, -1)
            tell(1, -1)

        return carry

    lax.fori_loop(jnp.where(helps, -1, 0), jnp.where(even, WINDOW, WINDOW - 1), pair, 0)

    @pl.when(jnp.logical_not(even))
    def _():
        def single(p, carry):
            lax.fori_loop(jnp.maximum(p, first_join), p + 1, join, 0)
            stages(1, p)
            return carry

        lax.fori_loop(rois - SLOTS, rois, single, 0)
        spread(WINDOW - 1, outgoing.at[0])

    out[0:SLOTS] = outgoing[0]
    for f in range(1, WINDOW):
        mask(f).wait_recv()

    out[SLOTS : 2 * SLOTS] = incoming[1] + outgoing[WINDOW]
    for f in range(2, WINDOW):
        out[f * SLOTS : (f + 1) * SLOTS] = incoming[f]

    for f in range(1, WINDOW):
        mask(f).wait_send()

    @pl.when(cut)
    def _():
        low_copy.wait_send()

    @pl.when(has_down)
    def _():
        smalls[0].wait_send()
        row_copy.wait_send()

    @pl.when(has_up)
    def _():
        smalls[1].wait_send()

        def drain(p, carry):
            piece(p).wait_send()
            return carry

        lax.fori_loop(first_sent, rois, drain, 0)


def body(
    count,
    features,
    corners,
    offsets,
    counts,
    classes,
    fpn_weight,
    head_weight,
    deconv_weight,
    class_weight,
):
    band_rows, columns, chans = features.shape
    rois = corners.shape[0]
    spots = corners.T
    turns = offsets.T
    smem = pl.BlockSpec(memory_space=pltpu.SMEM)
    vmem = pl.BlockSpec(memory_space=pltpu.VMEM)
    anyw = pl.BlockSpec(memory_space=pl.ANY)
    return pl.pallas_call(
        functools.partial(kernel, count),
        out_shape=jax.ShapeDtypeStruct((WINDOW * SLOTS, 4 * CELLS), F32),
        in_specs=[smem, smem, smem, smem, anyw, anyw, anyw, anyw, vmem],
        out_specs=vmem,
        scratch_shapes=[
            pltpu.VMEM(features.shape, BF16),
            pltpu.VMEM((chans // 128, band_rows, columns + 2 * EDGE, 128), F32),
            pltpu.VMEM(fpn_weight.shape, BF16),
            pltpu.VMEM(head_weight.shape, BF16),
            pltpu.VMEM(deconv_weight.shape, BF16),
            pltpu.VMEM(deconv_weight.shape[::-1], BF16),
            pltpu.SMEM((rois,), jnp.int32),
            pltpu.SMEM((1, rois + 3 * SLOTS), jnp.int32),
            pltpu.SMEM((2, 1, rois + 3 * SLOTS), jnp.int32),
            pltpu.SMEM((5, rois + SLOTS), jnp.int32),
            pltpu.VMEM((rois, band_rows + 2, SIDE, chans), BF16),
            pltpu.VMEM((rois, band_rows + 2, SIDE, chans), BF16),
            pltpu.VMEM((rois + 1, SIDE, chans), BF16),
            pltpu.VMEM((rois + 1, SIDE, chans), BF16),
            pltpu.VMEM((SLOTS * LOW + 1, SIDE, chans), BF16),
            pltpu.VMEM((SLOTS * LOW + 1, SIDE, chans), BF16),
            pltpu.VMEM((2, SIDE, chans), F32),
            pltpu.VMEM((SIDE, 2 * SIDE, chans), F32),
            pltpu.VMEM((rois + SLOTS, 3, 2 * band_rows + 1, SIDE, chans), BF16),
            pltpu.VMEM((SLOTS, SIDE, 2 * SIDE, chans), F32),
            pltpu.VMEM((3, SLOTS, SIDE + 2, SIDE, chans), BF16),
            pltpu.VMEM((SLOTS * CELLS, chans), BF16),
            pltpu.VMEM((rois + SLOTS, 4, CELLS), F32),
            pltpu.VMEM((WINDOW + 1, SLOTS, 4 * CELLS), F32),
            pltpu.VMEM((WINDOW, SLOTS, 4 * CELLS), F32),
            pltpu.SemaphoreType.DMA((CHUNKS + 5,)),
            pltpu.SemaphoreType.DMA((5,)),
            pltpu.SemaphoreType.DMA((5,)),
            pltpu.SemaphoreType.DMA((rois,)),
            pltpu.SemaphoreType.DMA((rois,)),
            pltpu.SemaphoreType.DMA((WINDOW,)),
            pltpu.SemaphoreType.DMA((WINDOW,)),
            pltpu.SemaphoreType.REGULAR((3,)),
        ],
        compiler_params=pltpu.CompilerParams(
            collective_id=0, has_side_effects=True, vmem_limit_bytes=60 * 1024 * 1024
        ),
    )(
        spots,
        turns,
        counts,
        classes,
        features,
        fpn_weight,
        head_weight,
        deconv_weight,
        class_weight,
    )


def solution(mesh):
    placed = (
        P(("tiles", "rows"), None, None),
        P(("tiles", "rows"), None),
        P(("tiles", "rows"), None),
        P(("tiles", "rows")),
        P(("tiles", "rows")),
        P(),
        P(),
        P(),
        P(),
    )
    return jax.shard_map(
        functools.partial(body, mesh.shape["rows"]),
        mesh=mesh,
        in_specs=placed,
        out_specs=P(("tiles", "rows"), None),
        check_vma=False,
    )
```
